32 devices in a mesh: job: 2 (over y), vocab: 4 (over x, core), req: 4 (over z).
Axes of the slice: x: 2, y: 2, z: 4, core: 2. Of those that a mesh axis runs over, the one named last changes fastest.
Arguments:
- target_hidden: bfloat16 [128, 5120], P(('job', 'req'), 'vocab'), parts along dimension 0, may hold values from -500 to 500
- target_gain: bfloat16 [10240], P('job'), parts along dimension 0, may hold values from 0.5 to 1.5
- target_head: bfloat16 [10240, 4096], P('job', ('vocab', 'req')), parts along dimension 0, may hold values from -5 to 5
- draft_input: bfloat16 [128, 2048], P(('job', 'req')), parts along dimension 0, may hold values from -60 to 60
- attn_gain: bfloat16 [4096], P('job'), parts along dimension 0, may hold values from 0.25 to 1.75
- query_proj: bfloat16 [4096, 2048], P(('job', 'req'), 'vocab'), parts along dimension 0, may hold values from -0.13258252 to 0.13258252
- keyval_proj: bfloat16 [4096, 1024], P(('job', 'req'), 'vocab'), parts along dimension 0, may hold values from -3.535534 to 3.535534
- output_proj: bfloat16 [4096, 2048], P(('job', 'vocab'), 'req'), parts along dimension 0, may hold values from -0.125 to 0.125
- draft_gain: bfloat16 [4096], P('job'), parts along dimension 0, may hold values from 0.25 to 1.75
- draft_head: bfloat16 [4096, 4096], P('job', ('vocab', 'req')), parts along dimension 0, may hold values from -5 to 5
- parents: int32 [128], P(('job', 'req')), parts along dimension 0, may hold values from 0 to 14, as said below
- token_ids: int32 [128], P('job'), parts along dimension 0, may hold values from 0 to 4095
- valid_counts: int32 [8], P('job'), parts along dimension 0, may hold values from 8 to 16, as said below
Outputs:
- mean_loss: float32 [2], P('job'), parts along dimension 0
- grad_head: bfloat16 [4096, 4096], P('job', ('vocab', 'req')), parts along dimension 0
- grad_gain: float32 [4096], P(('job', 'vocab')), parts along dimension 0
- grad_query: bfloat16 [4096, 2048], P(('job', 'req'), 'vocab'), parts along dimension 0
- grad_keyval: bfloat16 [4096, 1024], P(('job', 'req'), 'vocab'), parts along dimension 0
- grad_output: bfloat16 [4096, 2048], P(('job', 'vocab'), 'req'), parts along dimension 0
The draws below stay inside these ranges and needn't reach their ends.
There are 2 independent parts, one for each index of `job`. The reference program is written for one: setup_inputs(seed, part) draws one part's arguments, and reference() takes and returns one part's arrays. A program takes and returns all parts, laid end to end along the dimension named above; each array names one. Nothing has to cross between parts.
Inputs may be any that keep to these rules, and one draw needn't show every extreme that they name: `parents`: within each request group of 16 rows (local indices), row 0 is its own parent and every other row's parent is an earlier row of the same group; in the first group the last row's parent is the row just before it. `valid_counts`: some group has all 16 rows scored and some group exactly half of them.
All inputs are finite; a program needn't handle non-finite values.
Results may differ from the reference program's by a relative error of at most 0.013.
The reference program's roundings to bfloat16 on the way count: a program that leaves them out, or rounds other values in their place, can miss the bound.
Values may be sent and summed in bfloat16 or wider, within the bound.
A program may use at most 64 MiB of HBM per device.

```python
import math
import jax
import jax.numpy as jnp
import numpy as np
from jax import lax

D_T = 5120
DD = 2048
HEADS = 32
KV_HEADS = 8
HEAD_DIM = 64
ROWS_DEV = 16
GROUPS = 4
ROWS = 64
VOCAB = 4096
QD = 2048
KVD = 1024


def log_scales(key, shape, lower, upper):
    return jnp.exp(jax.random.uniform(key, shape, minval=jnp.log(lower), maxval=jnp.log(upper))).astype(jnp.float32)


def query_base(key):
    values = jnp.clip(jax.random.normal(jax.random.fold_in(key, 21), (DD, QD)), -5.0, 5.0)
    return (values / DD ** 0.5).astype(jnp.float32)


def draw_target_hidden(key, part):
    base = jnp.clip(jax.random.normal(jax.random.fold_in(key, 1), (ROWS, D_T)), -5.0, 5.0)
    values = base * log_scales(jax.random.fold_in(key, 3), (ROWS, 1), 0.5, 2.0)
    return values.astype(jnp.bfloat16)


def draw_target_head(key, part):
    values = jnp.clip(jax.random.normal(jax.random.fold_in(key, 5), (D_T, VOCAB)), -5.0, 5.0) * (3.0 / D_T ** 0.5)
    return values.astype(jnp.bfloat16)


def draw_draft_input(key, part):
    base = jnp.clip(jax.random.normal(jax.random.fold_in(key, 6), (ROWS, DD)), -5.0, 5.0)
    values = base * log_scales(jax.random.fold_in(key, 7), (ROWS, 1), 0.5, 2.0)
    return values.astype(jnp.bfloat16)


def draw_draft_head(key, part):
    values = jnp.clip(jax.random.normal(jax.random.fold_in(key, 8), (DD, VOCAB)), -5.0, 5.0) * (3.0 / DD ** 0.5)
    return values.astype(jnp.bfloat16)


def draw_query_proj(key, part):
    return query_base(key).astype(jnp.bfloat16)


def draw_keyval_proj(key, part):
    values = jnp.clip(jax.random.normal(jax.random.fold_in(key, 22), (DD, KVD)), -5.0, 5.0) / DD ** 0.5
    return values.astype(jnp.bfloat16)


def draw_parents(key, part):
    local_index = jnp.tile(jnp.arange(ROWS_DEV, dtype=jnp.int32), GROUPS)
    drawn = jax.random.randint(jax.random.fold_in(key, 30), (ROWS,), 0, jnp.maximum(local_index, 1)).astype(jnp.int32)
    return drawn.at[ROWS_DEV - 1].set(ROWS_DEV - 2).astype(jnp.int32)


def draw_valid_counts(key, part):
    fewest_rows = ROWS_DEV // 2
    counts = jax.random.randint(jax.random.fold_in(key, 31), (GROUPS,), fewest_rows, ROWS_DEV + 1)
    fullest = jax.random.randint(jax.random.fold_in(key, 32), (), 0, GROUPS)
    fewest = (fullest + 1 + jax.random.randint(jax.random.fold_in(key, 33), (), 0, GROUPS - 1)) % GROUPS
    counts = counts.at[fullest].set(ROWS_DEV).at[fewest].set(fewest_rows)
    return counts.astype(jnp.int32)


def set_ends(entries, stream_key, smallest, high):
    index_at = [jax.random.randint(jax.random.fold_in(stream_key, axis), (), 0, length) for axis, length in enumerate(entries.shape)]
    main_axis = entries.shape.index(max(entries.shape))
    beside = index_at[:main_axis] + [(index_at[main_axis] + 1) % entries.shape[main_axis]] + index_at[main_axis + 1:]
    return entries.at[tuple(index_at)].set(smallest).at[tuple(beside)].set(high)


def block_levels(own_key, extent, split, low, top_value):
    level, own = 1.0, jax.random.fold_in(own_key, 6)
    for dim, parts in split:
        steps = jnp.exp(jax.random.uniform(jax.random.fold_in(own, dim), (parts,), jnp.float32, low / len(split), top_value / len(split)))
        level = level * jnp.repeat(steps, extent[dim] // parts).reshape([-1 if axis == dim else 1 for axis in range(len(extent))])
    return level


def cumulative_ranks(amount, skew):
    loads = [(1 << 20) // math.isqrt(grade ** skew) + 1 for grade in range(1, amount + 1)]
    spread = 1 + sum(loads) // (1 << 30)
    return np.cumsum(np.array([max(1, weight // spread) for weight in loads]))


def skewed_ids(own_key, extent, number_of, slope):
    listing = cumulative_ranks(number_of, slope)
    lot = jax.random.randint(jax.random.fold_in(own_key, 1), extent, 0, int(listing[number_of - 1]))
    rank = jnp.searchsorted(jnp.asarray(listing, jnp.int32), lot, side="right")
    return jax.random.permutation(jax.random.fold_in(own_key, 2), number_of)[rank].astype(jnp.int32)


def centred(key, extent, width, most, pieces=(), kind=jnp.bfloat16):
    level = block_levels(key, extent, pieces, -0.22, 0.18) if pieces else 1.0
    result = jax.random.normal(key, extent, jnp.float32) * width * level
    return jnp.minimum(jnp.maximum(result, -most), most).astype(kind)


def setup_inputs(seed: int = 0, part: int = 0) -> dict:
    key_of = jax.random.split(jax.random.key(seed), 14)
    part_splits = jax.random.split(jax.random.fold_in(key_of[13], part), 14)
    target_hidden = draw_target_hidden(jax.random.fold_in(jax.random.fold_in(key_of[13], part), 71), part)
    target_gain = jnp.clip(1.0 + 0.1 * jax.random.normal(part_splits[1], (D_T,), jnp.float32), 0.5, 1.5).astype(jnp.bfloat16)
    target_head = draw_target_head(jax.random.fold_in(jax.random.fold_in(key_of[13], part), 71), part)
    draft_input = draw_draft_input(jax.random.fold_in(jax.random.fold_in(key_of[13], part), 71), part)
    attn_gain = jnp.clip(1.0 + 0.15 * jax.random.normal(part_splits[4], (DD,), jnp.float32), 0.25, 1.75).astype(jnp.bfloat16)
    query_proj = draw_query_proj(jax.random.fold_in(jax.random.fold_in(key_of[13], part), 71), part)
    keyval_proj = draw_keyval_proj(jax.random.fold_in(jax.random.fold_in(key_of[13], part), 71), part)
    output_proj = centred(part_splits[7], (QD, DD), QD ** -0.5, 0.125, ((0, 4), (1, 4)))
    draft_gain = jnp.clip(1.0 + 0.15 * jax.random.normal(part_splits[8], (DD,), jnp.float32), 0.25, 1.75).astype(jnp.bfloat16)
    draft_head = draw_draft_head(jax.random.fold_in(jax.random.fold_in(key_of[13], part), 71), part)
    parents = draw_parents(jax.random.fold_in(jax.random.fold_in(key_of[13], part), 71), part)
    token_ids = set_ends(skewed_ids(part_splits[11], (ROWS,), VOCAB, 2), jax.random.fold_in(part_splits[11], 3), 0, VOCAB - 1).astype(jnp.int32)
    valid_counts = draw_valid_counts(jax.random.fold_in(jax.random.fold_in(key_of[13], part), 71), part)
    return {"target_hidden": target_hidden, "target_gain": target_gain, "target_head": target_head, "draft_input": draft_input, "attn_gain": attn_gain, "query_proj": query_proj, "keyval_proj": keyval_proj, "output_proj": output_proj, "draft_gain": draft_gain, "draft_head": draft_head, "parents": parents, "token_ids": token_ids, "valid_counts": valid_counts}


epsilon = 1e-05
rope_base = 500000.0
hard_weight = 0.5
loss_scale = 1024.0

def rms_scale(values):
    return lax.rsqrt(lax.optimization_barrier(jnp.mean(values * values, axis=-1, keepdims=True)) + epsilon)

def ancestry(parent_rows):
    row_width = parent_rows.shape[-1]
    indices = jnp.arange(row_width, dtype=jnp.int32)
    links = (parent_rows[..., :, None] == indices).astype(jnp.float32)
    linked = jnp.maximum(links, jnp.eye(row_width, dtype=jnp.float32))
    for doubling in range(max(1, (row_width - 1).bit_length())):
        linked = jnp.minimum(jnp.matmul(linked, linked, precision=lax.Precision.HIGHEST), 1.0)
    return linked

def rotation(tree_depth, head_width):
    half_width = head_width // 2
    frequency = rope_base ** (-2.0 * jnp.arange(half_width, dtype=jnp.float32) / head_width)
    angles = tree_depth[:, None] * frequency[None, :]
    return (jnp.cos(angles), jnp.sin(angles))

def rotate(values, cosine, sine_table):
    half_width = values.shape[-1] // 2
    leading = values[..., :half_width]
    trailing = values[..., half_width:]
    cos_rows = cosine[:, None, :]
    sin_rows = sine_table[:, None, :]
    return jnp.concatenate([leading * cos_rows - trailing * sin_rows, trailing * cos_rows + leading * sin_rows], axis=-1)

def unrotate(gradient, cosine, sine_table):
    half_width = gradient.shape[-1] // 2
    leading = gradient[..., :half_width]
    trailing = gradient[..., half_width:]
    cos_rows = cosine[:, None, :]
    sin_rows = sine_table[:, None, :]
    return jnp.concatenate([leading * cos_rows + trailing * sin_rows, trailing * cos_rows - leading * sin_rows], axis=-1)

def attend(queries, key_rows, value_rows, ancestors):
    inv_root = queries.shape[-1] ** (-0.5)
    scores = jnp.einsum('ihd,jhd->hij', queries.astype(jnp.float32), key_rows.astype(jnp.float32)) * inv_root
    allowed = ancestors[None, :, :] > 0.5
    scores = jnp.where(allowed, scores, -jnp.inf)
    row_top = lax.optimization_barrier(jnp.max(scores, axis=-1, keepdims=True))
    powers = jnp.exp(scores - row_top)
    attn_probs = powers / lax.optimization_barrier(jnp.sum(powers, axis=-1, keepdims=True))
    attn_weights = attn_probs.astype(jnp.bfloat16)
    head_mix = jnp.einsum('hij,jhd->ihd', attn_weights.astype(jnp.float32), value_rows.astype(jnp.float32)).astype(jnp.bfloat16)
    return (attn_probs, attn_weights, head_mix)

def attend_back(mix_back, queries, key_rows, value_rows, attn_probs, attn_weights):
    inv_root = queries.shape[-1] ** (-0.5)
    prob_back = jnp.einsum('ihd,jhd->hij', mix_back.astype(jnp.float32), value_rows.astype(jnp.float32))
    value_back = jnp.einsum('hij,ihd->jhd', attn_weights.astype(jnp.float32), mix_back.astype(jnp.float32))
    row_delta = lax.optimization_barrier(jnp.sum(attn_probs * prob_back, axis=-1, keepdims=True))
    score_back = (attn_probs * (prob_back - row_delta) * inv_root).astype(jnp.bfloat16)
    query_back = jnp.einsum('hij,jhd->ihd', score_back.astype(jnp.float32), key_rows.astype(jnp.float32))
    key_back = jnp.einsum('hij,ihd->jhd', score_back.astype(jnp.float32), queries.astype(jnp.float32))
    return (query_back, key_back, value_back)

def by_group(values):
    return values.reshape((GROUPS, ROWS_DEV) + values.shape[1:])

def group_sum(left, right):
    left_groups = left.reshape(GROUPS, ROWS_DEV, left.shape[1])
    right_groups = right.reshape(GROUPS, ROWS_DEV, right.shape[1])

    def add_group(running, pair_rows):
        group_part = jnp.dot(pair_rows[0].T, pair_rows[1], preferred_element_type=jnp.float32)
        rounded = lax.optimization_barrier(group_part.astype(jnp.bfloat16))
        return (running + rounded.astype(jnp.float32), None)
    initial = jnp.zeros((left.shape[1], right.shape[1]), jnp.float32)
    running, unused = lax.scan(add_group, initial, (left_groups, right_groups))
    return running

def reference(target_hidden, target_gain, target_head, draft_input, attn_gain, query_proj, keyval_proj, output_proj, draft_gain, draft_head, parents, token_ids, valid_counts):
    head_group = HEADS // KV_HEADS
    target_rows = target_hidden.astype(jnp.float32)
    normed_target = (target_rows * rms_scale(target_rows) * target_gain.astype(jnp.float32)).astype(jnp.bfloat16)
    target_logits = jnp.dot(normed_target, target_head, preferred_element_type=jnp.float32)
    ancestors = ancestry(parents.reshape(GROUPS, ROWS_DEV))
    tree_depth = (lax.optimization_barrier(jnp.sum(ancestors, axis=-1)) - 1.0).reshape(ROWS)
    cosine, sine_table = rotation(tree_depth, HEAD_DIM)
    inputs = draft_input.astype(jnp.float32)
    normed_input = (inputs * rms_scale(inputs) * attn_gain.astype(jnp.float32)).astype(jnp.bfloat16)
    query_raw = jnp.dot(normed_input, query_proj, preferred_element_type=jnp.float32).reshape(ROWS, HEADS, HEAD_DIM)
    queries = rotate(query_raw, cosine, sine_table).astype(jnp.bfloat16)
    projected = jnp.dot(normed_input, keyval_proj, preferred_element_type=jnp.float32).reshape(ROWS, 2, KV_HEADS, HEAD_DIM)
    key_rows = rotate(projected[:, 0], cosine, sine_table).astype(jnp.bfloat16)
    value_rows = projected[:, 1].astype(jnp.bfloat16)
    key_wide = jnp.repeat(key_rows, head_group, axis=1)
    value_wide = jnp.repeat(value_rows, head_group, axis=1)
    attn_probs, attn_weights, head_mix = jax.vmap(attend)(by_group(queries), by_group(key_wide), by_group(value_wide), ancestors)
    head_mix = head_mix.reshape(ROWS, HEADS * HEAD_DIM)
    attn_out = jnp.dot(head_mix, output_proj, preferred_element_type=jnp.float32)
    hidden = inputs + attn_out
    hidden_scale = rms_scale(hidden)
    hidden_norm = hidden * hidden_scale
    normed_draft = (hidden_norm * draft_gain.astype(jnp.float32)).astype(jnp.bfloat16)
    draft_logits = jnp.dot(normed_draft, draft_head, preferred_element_type=jnp.float32)
    target_top = lax.optimization_barrier(jnp.max(target_logits, axis=1))
    target_pow = jnp.exp(target_logits - target_top[:, None])
    target_total = lax.optimization_barrier(jnp.sum(target_pow, axis=1))
    cross_total = lax.optimization_barrier(jnp.sum(target_pow * (target_logits - draft_logits), axis=1))
    draft_top = lax.optimization_barrier(jnp.max(draft_logits, axis=1))
    draft_pow = jnp.exp(draft_logits - draft_top[:, None])
    draft_total = lax.optimization_barrier(jnp.sum(draft_pow, axis=1))
    onehot = token_ids[:, None] == jnp.arange(VOCAB, dtype=jnp.int32)[None, :]
    token_logit = lax.optimization_barrier(jnp.sum(jnp.where(onehot, draft_logits, 0.0), axis=1))
    target_lse = target_top + jnp.log(target_total)
    draft_lse = draft_top + jnp.log(draft_total)
    row_loss = cross_total / target_total - target_lse + draft_lse + hard_weight * (draft_lse - token_logit)
    valid_rows = (jnp.arange(ROWS_DEV, dtype=jnp.int32)[None, :] < valid_counts[:, None]).astype(jnp.float32).reshape(ROWS)
    valid_total = jnp.sum(valid_counts).astype(jnp.float32)
    mean_loss = (jnp.sum(valid_rows * row_loss) / valid_total).reshape(1)
    target_prob = target_pow / target_total[:, None]
    draft_prob = draft_pow / draft_total[:, None]
    row_coef = loss_scale * valid_rows / valid_total
    logit_back = (row_coef[:, None] * ((1.0 + hard_weight) * draft_prob - target_prob - hard_weight * onehot.astype(jnp.float32))).astype(jnp.bfloat16)
    grad_head = jnp.dot(normed_draft.T, logit_back, preferred_element_type=jnp.float32).astype(jnp.bfloat16)
    row_back = jnp.dot(logit_back, draft_head.T, preferred_element_type=jnp.float32)
    grad_gain = lax.optimization_barrier(jnp.sum(row_back * hidden_norm, axis=0))
    scaled_back = row_back * draft_gain.astype(jnp.float32)
    hidden_back = hidden_scale * (scaled_back - hidden_norm * lax.optimization_barrier(jnp.mean(scaled_back * hidden_norm, axis=-1, keepdims=True)))
    out_back = hidden_back.astype(jnp.bfloat16)
    grad_output = group_sum(head_mix, out_back)
    mix_back = jnp.dot(out_back, output_proj.T, preferred_element_type=jnp.float32).astype(jnp.bfloat16).reshape(ROWS, HEADS, HEAD_DIM)
    query_back, key_back, value_back = jax.vmap(attend_back)(by_group(mix_back), by_group(queries), by_group(key_wide), by_group(value_wide), attn_probs, attn_weights)
    query_back = unrotate(query_back.reshape(ROWS, HEADS, HEAD_DIM), cosine, sine_table).astype(jnp.bfloat16).reshape(ROWS, HEADS * HEAD_DIM)
    key_back = unrotate(key_back.reshape(ROWS, KV_HEADS, head_group, HEAD_DIM).sum(axis=2), cosine, sine_table)
    value_back = value_back.reshape(ROWS, KV_HEADS, head_group, HEAD_DIM).sum(axis=2)
    keyval_back = jnp.stack([key_back, value_back], axis=1).astype(jnp.bfloat16).reshape(ROWS, 2 * KV_HEADS * HEAD_DIM)
    grad_query = group_sum(normed_input, query_back)
    grad_keyval = group_sum(normed_input, keyval_back)
    return (mean_loss, grad_head, grad_gain, grad_query.astype(jnp.bfloat16), grad_keyval.astype(jnp.bfloat16), grad_output.astype(jnp.bfloat16))
```

```python
import functools
import math

import jax
import jax.numpy as jnp
from jax import lax
from jax.experimental import pallas as pl
from jax.experimental.pallas import tpu as pltpu
from jax.sharding import PartitionSpec as P

HEADS = 32
KV_HEADS = 8
HEAD_DIM = 64

epsilon = 1e-05
rope_base = 500000.0
hard_weight = 0.5
loss_scale = 1024.0
f32 = jnp.float32
bf16 = jnp.bfloat16
MESH = pl.DeviceIdType.MESH


def dot_nn(a, b):
    return jnp.dot(a, b, preferred_element_type=f32)


def dot_tn(a, b):
    return lax.dot_general(a, b, (((0,), (0,)), ((), ())), preferred_element_type=f32)


def dot_nt(a, b):
    return lax.dot_general(a, b, (((1,), (1,)), ((), ())), preferred_element_type=f32)


def as_row(ref, first, count):
    lanes = ref.shape[1]
    values = ref[...].astype(f32)
    rows = range(first // lanes, (first + count) // lanes)
    return jnp.concatenate([values[k : k + 1] for k in rows], axis=1)


def grouped(lhs, rhs, out, groups, step):
    for first in range(0, out.shape[0], step):
        value = None
        for g in range(groups):
            term = dot_tn(lhs(g, first, step), rhs(g)).astype(bf16).astype(f32)
            value = term if value is None else value + term
        out[first : first + step] = value.astype(bf16)


def total(ref, count):
    value = ref[0]
    for k in range(1, count):
        value = value + ref[k]
    return value


def swap_halves(values):
    width = values.shape[1]
    half = HEAD_DIM // 2
    lane = lax.broadcasted_iota(jnp.int32, values.shape, 1)
    if width % 128 == 0:
        ahead = pltpu.roll(values, width - half, 1)
        behind = pltpu.roll(values, half, 1)
        return jnp.where(lane % HEAD_DIM < half, -ahead, behind)
    pieces = []
    for head in range(width // HEAD_DIM):
        lead = values[:, head * HEAD_DIM : head * HEAD_DIM + half]
        trail = values[:, head * HEAD_DIM + half : (head + 1) * HEAD_DIM]
        pieces += [-trail, lead]
    return jnp.concatenate(pieces, axis=1)


def angles(depth, rows, width):
    lane = lax.broadcasted_iota(jnp.int32, (rows, width), 1) % (HEAD_DIM // 2)
    frequency = jnp.exp(lane.astype(f32) * (-2.0 / HEAD_DIM * math.log(rope_base)))
    return depth * frequency


def group_of(v, V):
    return v // 2 * (1 - v % 2) + (V - 1 - v // 2) * (v % 2)


def owner_of(group, V):
    upper = group // (V // 2)
    return 2 * group * (1 - upper) + (2 * (V - 1 - group) + 1) * upper


def step_kernel(
    V,
    R,
    target_hidden,
    target_gain,
    target_head,
    draft_input,
    attn_gain,
    query_proj,
    keyval_proj,
    output_proj,
    draft_gain,
    draft_head,
    parents,
    token_ids,
    valid_counts,
    mean_loss,
    grad_head,
    grad_gain,
    grad_output,
    grad_query,
    x_rows,
    keyval_rows,
    w_target,
    w_query,
    w_keyval,
    wd,
    wo,
    head_block,
    output_block,
    query_block,
    t_gain,
    t1,
    t2,
    d_out,
    d_in,
    x_out,
    x_in,
    k_out,
    k_in,
    a_out,
    a_in,
    mix,
    hm,
    hid,
    hnorm,
    gains,
    nd,
    dl,
    tl_out,
    tl_in,
    stat_all,
    loss_all,
    lb_out,
    lb_in,
    b_out,
    b_in,
    c_out,
    c_in,
    ob,
    m_out,
    m_in,
    gain_out,
    gain_in,
    kv_out,
    kv_in,
    qg,
    local_sems,
    send_sems,
    recv_sems,
    k_sems,
    hm_sems,
    m_sems,
    gain_sems,
    kv_sems,
    stat_sems,
):
    v = lax.axis_index("vocab")
    r = lax.axis_index("req")
    half = V // 2
    chip, core = v // 2, lax.rem(v, 2)
    sibling = v + 1 - 2 * core
    group = group_of(v, V)
    rows = draft_input.shape[0]
    width = draft_input.shape[1]
    all_rows = rows * R
    n = rows * half
    part = width // R
    qcols = query_proj.shape[1]
    kcols = keyval_proj.shape[1]
    vocab_width = draft_head.shape[1]
    t_part = target_hidden.shape[1]
    t_width = t_part * V
    local_heads = qcols // HEAD_DIM
    head_group = HEADS // KV_HEADS
    shared = max(1, local_heads // head_group)
    spread = local_heads // shared
    swidth = shared * HEAD_DIM
    pieces = kcols // swidth
    inv_root = HEAD_DIM ** (-0.5)

    loads = []
    for index, (source, target) in enumerate(
        (
            (query_proj, w_query),
            (keyval_proj, w_keyval),
            (target_head, w_target),
            (output_proj, wo.at[v]),
            (draft_head, wd.at[core]),
        )
    ):
        load = pltpu.make_async_copy(source, target, local_sems.at[index])
        load.start()
        loads.append(load)

    barrier = pltpu.get_barrier_semaphore()
    for dv in range(V):
        for dr in range(R):
            if dv or dr:
                pl.semaphore_signal(
                    barrier,
                    inc=1,
                    device_id={"vocab": lax.rem(v + dv, V), "req": lax.rem(r + dr, R)},
                    device_id_type=MESH,
                )

    sent, sent_unless = [], []
    used = [0, 0]

    def describe(source, target, device, recv):
        used[0] += 1
        return pltpu.make_async_remote_copy(
            src_ref=source,
            dst_ref=target,
            send_sem=send_sems.at[used[0] - 1],
            recv_sem=recv,
            device_id=device,
            device_id_type=MESH,
        )

    def push(source, target, device, recv=None):
        if recv is None:
            recv = recv_sems.at[used[1]]
            used[1] += 1
        copy = describe(source, target, device, recv)
        copy.start()
        sent.append(copy)
        return copy

    def push_unless(here, source, target, device, recv):
        copy = describe(source, target, device, recv)

        @pl.when(jnp.logical_not(here))
        def _():
            copy.start()

        @pl.when(here)
        def _():
            pltpu.make_async_copy(source, target, recv).start()

        sent_unless.append((copy, here))

    def landed(target, recv):
        pltpu.make_async_remote_copy(
            src_ref=target,
            dst_ref=target,
            send_sem=recv,
            recv_sem=recv,
            device_id={"vocab": sibling},
            device_id_type=MESH,
        ).wait_recv()

    def over_req(source, target):
        peers = [lax.rem(r + k, R) for k in range(1, R)]
        return [push(source(p), target.at[r], {"req": p}) for p in peers]

    def over_chips(source, target):
        chips = [lax.rem(chip + k, half) for k in range(1, half)]
        return [push(source(c), target, {"vocab": 2 * c + core}) for c in chips]

    def arrive(copies):
        for copy in copies:
            copy.wait_recv()

    inputs = draft_input[...].astype(f32)
    scale = lax.rsqrt(jnp.mean(inputs * inputs, axis=-1, keepdims=True) + epsilon)
    normed = (inputs * scale * as_row(attn_gain, 0, width)).astype(bf16)
    for p in range(R):
        x_out[p] = normed[:, p * part : (p + 1) * part]
        d_out[p] = draft_input[:, p * part : (p + 1) * part]
    x_in[r] = x_out[r]
    t1[r] = target_hidden[...]

    row_i = lax.broadcasted_iota(jnp.int32, (rows, rows), 0)
    col_i = lax.broadcasted_iota(jnp.int32, (rows, rows), 1)
    eye = row_i == col_i
    parent_col = jnp.sum(
        jnp.where(eye, parents[...].astype(f32), 0.0), axis=1, keepdims=True
    )
    linked = jnp.where(
        jnp.logical_or(eye, parent_col == col_i.astype(f32)), 1.0, 0.0
    ).astype(f32)
    for doubling in range(max(1, (rows - 1).bit_length())):
        half_linked = linked.astype(bf16)
        linked = jnp.minimum(dot_nn(half_linked, half_linked), 1.0)
    depth = jnp.sum(linked, axis=1, keepdims=True) - 1.0
    pl.semaphore_wait(barrier, V * R - 1)
    got_x = over_req(lambda p: x_out.at[p], x_in)
    got_wo = over_chips(lambda c: output_proj, wo.at[v])
    got_wo_near = push(output_proj, wo.at[v], {"vocab": sibling})
    got_wd = push(draft_head, wd.at[core], {"vocab": sibling})
    here = r == group
    d_sems = []
    for k in range(1, R):
        p = lax.rem(r + k, R)
        copy = describe(d_out.at[p], d_in, {"req": p}, local_sems.at[8])

        @pl.when(here)
        def _():
            copy.start()

        sent_unless.append((copy, jnp.logical_not(here)))

    @pl.when(here)
    def _():
        d_in[...] = d_out[r]

    table = min(qcols, 128)
    angle = angles(depth, rows, table)
    q_cos = jnp.concatenate([jnp.cos(angle)] * (qcols // table), axis=1)
    q_sin = jnp.concatenate([jnp.sin(angle)] * (qcols // table), axis=1)
    s_cos, s_sin = q_cos[:, :swidth], q_sin[:, :swidth]

    loads[1].wait()
    arrive(got_x)
    x_all = x_in[...].reshape(all_rows, part)
    kv_part = dot_nn(x_all, w_keyval[...])
    for piece in range(pieces):
        k_out[piece] = kv_part[:, piece * swidth : (piece + 1) * swidth].reshape(
            R, rows, swidth
        )
    kind = v // half
    for k in range(R):
        p = lax.rem(r + k, R)
        for d in range(2):
            target_v = lax.rem(v, half) * 2 + d
            push_unless(
                jnp.logical_and(target_v == v, p == r),
                k_out.at[d * pieces // 2, p],
                k_in.at[kind, r],
                {"vocab": target_v, "req": p},
                k_sems.at[kind, r],
            )
    loads[0].wait()
    a_out[...] = dot_nn(x_all, w_query[...]).reshape(R, rows, qcols)
    got_a = over_req(lambda p: a_out.at[p], a_in)
    a_in[r] = a_out[r]
    got_t1 = over_req(lambda p: t1.at[r], t1)
    x_rows[...] = x_in[...]

    for p in range(R):
        gains[p] = as_row(draft_gain, p * part, part)
    t_gain[...] = as_row(target_gain, 0, t_width)

    big_row = lax.broadcasted_iota(jnp.int32, (n, n), 0)
    big_col = lax.broadcasted_iota(jnp.int32, (n, n), 1)
    diagonal = big_row == big_col

    def to_col(row):
        return jnp.sum(jnp.where(diagonal, row, 0.0), axis=1, keepdims=True)

    def to_row(col):
        return jnp.sum(jnp.where(diagonal, col, 0.0), axis=0, keepdims=True)

    def groups_of(index):
        place = index // rows
        return place * (1 - core) + (V - 1 - place) * core

    token_row = lax.broadcasted_iota(jnp.int32, (n, all_rows), 0)
    token_at = lax.broadcasted_iota(jnp.int32, (n, all_rows), 1)
    token_col = jnp.sum(
        jnp.where(
            groups_of(token_row) * rows + token_row % rows == token_at,
            token_ids[...].astype(f32),
            0.0,
        ),
        axis=1,
        keepdims=True,
    )
    lane = lax.broadcasted_iota(jnp.int32, (n, 2 * vocab_width), 1)
    lane_block = lane // vocab_width
    columns = ((2 * chip + lane_block) * R + r) * vocab_width + lane % vocab_width
    onehot = token_col == columns.astype(f32)
    counts = valid_counts[...].astype(f32)
    group_row = lax.broadcasted_iota(jnp.int32, (n, R), 0)
    group_col = lax.broadcasted_iota(jnp.int32, (n, R), 1)
    count_col = jnp.sum(
        jnp.where(groups_of(group_row) == group_col, counts, 0.0), axis=1, keepdims=True
    )
    local_row = (lax.broadcasted_iota(jnp.int32, (n, 1), 0) % rows).astype(f32)
    valid = jnp.where(local_row < count_col, 1.0, 0.0)
    valid_row = to_row(valid)
    valid_total = jnp.sum(counts, axis=1, keepdims=True)

    for p in range(R):
        for which in range(2):
            landed(k_in.at[which, p], k_sems.at[which, p])
    key_raw = total(k_in.at[0], R)
    key_rows = (key_raw * s_cos + swap_halves(key_raw) * s_sin).astype(bf16)
    value_rows = total(k_in.at[1], R).astype(bf16)
    arrive(got_a)
    query_raw = total(a_in, R)
    queries = (query_raw * q_cos + swap_halves(query_raw) * q_sin).astype(bf16)

    def stack_heads(values, group):
        return jnp.concatenate(
            [
                values[:, (group * spread + h) * HEAD_DIM : (group * spread + h + 1) * HEAD_DIM]
                for h in range(spread)
            ],
            axis=0,
        )

    def unstack_heads(stacks):
        return jnp.concatenate(
            [stack[h * rows : (h + 1) * rows] for stack in stacks for h in range(spread)],
            axis=1,
        )

    query_stacks = [stack_heads(queries, s) for s in range(shared)]
    allowed = jnp.concatenate([linked] * spread, axis=0) > 0.5
    probs, weights, keys, values, mixes = [], [], [], [], []
    for s in range(shared):
        key = key_rows[:, s * HEAD_DIM : (s + 1) * HEAD_DIM]
        value = value_rows[:, s * HEAD_DIM : (s + 1) * HEAD_DIM]
        scores = dot_nt(query_stacks[s], key) * inv_root
        scores = jnp.where(allowed, scores, -jnp.inf)
        powers = jnp.exp(scores - jnp.max(scores, axis=-1, keepdims=True))
        prob = powers / jnp.sum(powers, axis=-1, keepdims=True)
        weight = prob.astype(bf16)
        probs.append(prob)
        weights.append(weight)
        keys.append(key)
        values.append(value)
        mixes.append(dot_nn(weight, value))
    mix[r] = unstack_heads(mixes).astype(bf16)
    owner = owner_of(r, V)
    for k in range(R):
        p = lax.rem(r + k, R)
        push_unless(
            jnp.logical_and(owner == v, p == r),
            mix.at[r],
            hm.at[v],
            {"vocab": owner, "req": p},
            hm_sems.at[v],
        )

    arrive(got_wo)
    got_wo_pass = []
    for k in range(1, half):
        sender = lax.rem(v + V - 2 * k, V)
        got_wo_pass.append(push(wo.at[sender], wo.at[sender], {"vocab": sibling}))
    arrive(got_t1)
    t2[v] = t1[...]
    got_t2_far = over_chips(lambda c: t2.at[v], t2.at[v])
    got_t2_near = push(t2.at[v], t2.at[v], {"vocab": sibling})
    got_mix = over_req(lambda p: mix.at[r], mix)

    loads[3].wait()
    got_wo_near.wait_recv()
    @pl.when(jnp.logical_not(here))
    def _():
        landed(d_in, local_sems.at[8])

    value = d_in[...].astype(f32)
    for p in range(V):
        landed(hm.at[p], hm_sems.at[p])
    arrive(got_wo_pass)
    attn_out = None
    for p in range(V):
        term = dot_nn(hm[p], wo[p])
        attn_out = term if attn_out is None else attn_out + term
    hid[r] = value + attn_out
    got_h = over_req(lambda p: hid.at[r], hid)

    arrive(got_t2_far)
    got_pass = []
    for k in range(1, half):
        sender = lax.rem(v + V - 2 * k, V)
        got_pass.append(push(t2.at[sender], t2.at[sender], {"vocab": sibling}))
    loads[2].wait()
    got_t2_near.wait_recv()
    arrive(got_pass)
    squares = jnp.zeros((all_rows, 1), f32)
    for p in range(V):
        piece = t2[p].reshape(all_rows, t_part).astype(f32)
        squares = squares + jnp.sum(piece * piece, axis=-1, keepdims=True)
    t_scale = lax.rsqrt(squares / t_width + epsilon)

    def target_part(first, last):
        value = None
        for p in range(first, last):
            piece = t2[p].reshape(all_rows, t_part).astype(f32)
            piece = (piece * t_scale * t_gain[:, p * t_part : (p + 1) * t_part]).astype(bf16)
            term = dot_nn(piece, w_target[p * t_part : (p + 1) * t_part])
            value = term if value is None else value + term
        return value

    first_logits = target_part(0, half)

    arrive(got_h)
    squares = jnp.zeros((rows, 1), f32)
    for p in range(R):
        squares = squares + jnp.sum(hid[p] * hid[p], axis=-1, keepdims=True)
    hidden_scale = lax.rsqrt(squares / width + epsilon)
    for p in range(R):
        norm = hid[p] * hidden_scale
        hnorm[p] = norm
        nd[core, chip, :, p * part : (p + 1) * part] = (norm * gains[p]).astype(bf16)
    got_nd = over_chips(lambda c: nd.at[core, chip], nd.at[core, chip])
    tl_out[...] = (first_logits + target_part(half, V)).reshape(R, rows, vocab_width)
    got_tl = []
    for k in range(half):
        mine = k * (1 - core) + (V - 1 - k) * core
        other = k * core + (V - 1 - k) * (1 - core)
        got_tl.append(push(tl_out.at[other], tl_in.at[core, k], {"vocab": sibling}))
        tl_in[core, k] = tl_out[mine]
    loads[4].wait()
    got_wd.wait_recv()

    def draft_part(place):
        for b in range(2):
            dl[place, :, b * vocab_width : (b + 1) * vocab_width] = dot_nn(
                nd[core, place], wd[b]
            )

    draft_part(chip)
    arrive(got_tl)
    target_logits = jnp.concatenate(
        [tl_in[b].reshape(n, vocab_width) for b in range(2)], axis=1
    )
    t_max = jnp.max(target_logits, axis=1, keepdims=True)
    t_pow = jnp.exp(target_logits - t_max)
    t_sum = jnp.sum(t_pow, axis=1, keepdims=True)
    arrive(got_nd)
    for k in range(1, half):
        draft_part(lax.rem(chip + k, half))

    draft_logits = dl[...].reshape(n, 2 * vocab_width)
    d_max = jnp.max(draft_logits, axis=1, keepdims=True)
    d_pow = jnp.exp(draft_logits - d_max)
    stats = (
        t_max,
        d_max,
        t_sum,
        jnp.sum(t_pow * (target_logits - draft_logits), axis=1, keepdims=True),
        jnp.sum(d_pow, axis=1, keepdims=True),
        jnp.sum(jnp.where(onehot, draft_logits, 0.0), axis=1, keepdims=True),
    )
    stats = [to_row(item) for item in stats]
    stat_kind = lax.broadcasted_iota(jnp.int32, (8, n), 0)

    def pack(items):
        packed = jnp.zeros((8, n), f32)
        for index, item in enumerate(items):
            packed = jnp.where(stat_kind == index, item, packed)
        return packed

    def combine(ref, count):
        top = ref[0]
        for k in range(1, count):
            top = jnp.maximum(top, ref[k])
        t_top, d_top = top[0:1], top[1:2]
        t_sum, cross, d_sum, token = 0.0, 0.0, 0.0, 0.0
        for k in range(count):
            piece = ref[k]
            t_factor = jnp.exp(piece[0:1] - t_top)
            t_sum = t_sum + piece[2:3] * t_factor
            cross = cross + piece[3:4] * t_factor
            d_sum = d_sum + piece[4:5] * jnp.exp(piece[1:2] - d_top)
            token = token + piece[5:6]
        return t_top, d_top, t_sum, cross, d_sum, token

    place = chip * R + r
    stat_all[place] = pack(stats)
    got_stats = []
    for dc in range(half):
        for dr in range(R):
            if dc or dr:
                device = {
                    "vocab": 2 * lax.rem(chip + dc, half) + core,
                    "req": lax.rem(r + dr, R),
                }
                got_stats.append(
                    push(
                        stat_all.at[place],
                        stat_all.at[place],
                        device,
                        stat_sems.at[dc * R + dr],
                    )
                )
    got_nd_near = push(nd.at[core], nd.at[core], {"vocab": sibling})
    arrive(got_stats)
    t_top, d_top, target_total, cross_total, draft_total, token_logit = combine(
        stat_all, half * R
    )

    row_coef = loss_scale * valid / valid_total
    target_prob = t_pow * to_col(jnp.exp(stats[0] - t_top) / target_total)
    draft_prob = d_pow * to_col(jnp.exp(stats[1] - d_top) / draft_total)
    logit_back = (
        row_coef
        * (
            (1.0 + hard_weight) * draft_prob
            - target_prob
            - jnp.where(onehot, hard_weight, 0.0)
        )
    ).astype(bf16)

    for p in range(R):
        row_part = None
        for b in range(2):
            term = dot_nt(
                logit_back[:, b * vocab_width : (b + 1) * vocab_width],
                wd[b, p * part : (p + 1) * part],
            )
            row_part = term if row_part is None else row_part + term
        b_out[:, :, p * part : (p + 1) * part] = row_part.reshape(half, rows, part)
    got_b = over_chips(lambda c: b_out.at[c], b_in.at[chip])
    b_in[chip] = b_out[chip]
    for b in range(2):
        lb_out[b] = logit_back[:, b * vocab_width : (b + 1) * vocab_width]
    got_lb = push(lb_out.at[1 - core], lb_in.at[core], {"vocab": sibling})
    lb_in[core] = lb_out[core]
    target_lse = t_top + jnp.log(target_total)
    draft_lse = d_top + jnp.log(draft_total)
    row_loss = (
        cross_total / target_total
        - target_lse
        + draft_lse
        + hard_weight * (draft_lse - token_logit)
    )
    loss_all[core] = jnp.broadcast_to(
        jnp.sum(valid_row * row_loss, axis=1, keepdims=True), (8, 128)
    )
    got_loss = push(loss_all.at[core], loss_all.at[core], {"vocab": sibling})
    got_nd_near.wait_recv()
    got_lb.wait_recv()
    lb_all = lb_in[...].reshape(all_rows, vocab_width)
    for p in range(R):
        head_block[p * part : (p + 1) * part] = dot_tn(
            nd[:, :, :, p * part : (p + 1) * part].reshape(all_rows, part), lb_all
        ).astype(bf16)
    head_store = pltpu.make_async_copy(head_block, grad_head, local_sems.at[5])
    head_store.start()

    arrive(got_b)
    inner = jnp.zeros((rows, 1), f32)
    for p in range(R):
        piece = b_in[0, :, p * part : (p + 1) * part]
        for k in range(1, half):
            piece = piece + b_in[k, :, p * part : (p + 1) * part]
        c_out[p, :, :part] = piece
        inner = inner + jnp.sum(piece * gains[p] * hnorm[p], axis=-1, keepdims=True)
    for p in range(R):
        c_out[p, :, part:] = jnp.broadcast_to(inner, (rows, 128))
    got_c = over_req(lambda p: c_out.at[p], c_in)
    c_in[r] = c_out[r]
    got_loss.wait_recv()
    mean_loss[...] = (loss_all[0] + loss_all[1])[0:1, 0:1] / valid_total
    arrive(got_c)
    back = total(c_in, R)
    row_back = back[:, :part]
    inner = back[:, part : part + 1] / width
    norm = hnorm[r]
    out_back = (hidden_scale * (row_back * gains[r] - norm * inner)).astype(bf16)
    ob[v] = out_back
    for k in range(V):
        p = lax.rem(v + k, V)
        m_out[p] = dot_nt(out_back, wo[p])
        push_unless(
            jnp.logical_and(p == v, group == r),
            m_out.at[p],
            m_in.at[r],
            {"vocab": p, "req": group},
            m_sems.at[r],
        )
    got_ob = [
        push(ob.at[v], ob.at[v], {"vocab": lax.rem(v + k, V)}) for k in range(1, V)
    ]
    gain_out[...] = jnp.broadcast_to(jnp.sum(row_back * norm, axis=0, keepdims=True), (8, part))
    for k in range(R):
        p = lax.rem(r + k, R)
        push_unless(
            jnp.logical_and(r == v, p == r),
            gain_out,
            gain_in.at[v],
            {"vocab": r, "req": p},
            gain_sems.at[v],
        )

    arrive(got_mix)
    arrive(got_ob)
    grouped(
        lambda g, a, count: mix[g, :, a : a + count],
        lambda g: ob[owner_of(g, V)],
        output_block,
        R,
        128,
    )
    output_store = pltpu.make_async_copy(output_block, grad_output, local_sems.at[6])
    output_store.start()

    for p in range(R):
        landed(m_in.at[p], m_sems.at[p])
    mix_back = total(m_in, R).astype(bf16)
    query_parts, key_parts, value_parts = [], [], []
    for s in range(shared):
        back_stack = stack_heads(mix_back, s)
        prob_back = dot_nt(back_stack, values[s])
        delta = jnp.sum(probs[s] * prob_back, axis=-1, keepdims=True)
        score_back = (probs[s] * (prob_back - delta) * inv_root).astype(bf16)
        query_parts.append(dot_nn(score_back, keys[s]))
        key_parts.append(dot_tn(score_back, query_stacks[s]))
        value_parts.append(dot_tn(weights[s], back_stack))
    key_back = jnp.concatenate(key_parts, axis=1)
    key_back = key_back * s_cos - swap_halves(key_back) * s_sin
    kv_out[0] = key_back.astype(kv_out.dtype)
    kv_out[1] = jnp.concatenate(value_parts, axis=1).astype(kv_out.dtype)
    for k in range(R):
        p = lax.rem(r + k, R)
        for which in range(2):
            target_v = which * half + chip
            push_unless(
                jnp.logical_and(target_v == v, p == r),
                kv_out.at[which],
                kv_in.at[r, core],
                {"vocab": target_v, "req": p},
                kv_sems.at[r, core],
            )
    query_back = unstack_heads(query_parts)
    qg[r] = (query_back * q_cos - swap_halves(query_back) * q_sin).astype(bf16)
    got_qg = over_req(lambda p: qg.at[r], qg)

    for p in range(V):
        landed(gain_in.at[p], gain_sems.at[p])
    grad_gain[...] = total(gain_in, V)[0:1]
    arrive(got_qg)
    grouped(lambda g, a, count: x_in[g, :, a : a + count], lambda g: qg[g], query_block, R, 128)
    query_store = pltpu.make_async_copy(query_block, grad_query, local_sems.at[7])
    query_store.start()
    for p in range(R):
        for d in range(2):
            landed(kv_in.at[p, d], kv_sems.at[p, d])
        if pieces == 1:
            keyval_rows[p] = (kv_in[p, 0] + kv_in[p, 1]).astype(bf16)
        else:
            for d in range(2):
                keyval_rows[p, :, d * swidth : (d + 1) * swidth] = kv_in[p, d]
    query_store.wait()
    head_store.wait()
    output_store.wait()
    for copy in sent:
        copy.wait_send()
    for copy, here in sent_unless:

        @pl.when(jnp.logical_not(here))
        def _():
            copy.wait_send()


def finish_kernel(
    R,
    loss_in,
    head_in,
    gain_in,
    output_in,
    query_in,
    x_rows,
    keyval_rows,
    mean_loss,
    grad_head,
    grad_gain,
    grad_query,
    grad_keyval,
    grad_output,
    head_block,
    output_block,
    query_block,
    sems,
):
    moves = (
        (head_in, head_block, grad_head),
        (output_in, output_block, grad_output),
        (query_in, query_block, grad_query),
    )
    loads = [
        pltpu.make_async_copy(source, block, sems.at[k])
        for k, (source, block, _) in enumerate(moves)
    ]
    stores = [
        pltpu.make_async_copy(block, target, sems.at[3 + k])
        for k, (_, block, target) in enumerate(moves)
    ]
    for load in loads:
        load.start()
    mean_loss[...] = loss_in[...]
    grad_gain[...] = gain_in[...]
    for load, store in zip(loads, stores):
        load.wait()
        store.start()
    grouped(lambda g, a, n: x_rows[g, :, a : a + n], lambda g: keyval_rows[g], grad_keyval, R, 128)
    for store in stores:
        store.wait()


def shards(
    V,
    R,
    target_hidden,
    target_gain,
    target_head,
    draft_input,
    attn_gain,
    query_proj,
    keyval_proj,
    output_proj,
    draft_gain,
    draft_head,
    parents,
    token_ids,
    valid_counts,
):
    rows, width = draft_input.shape
    part = width // R
    qcols = query_proj.shape[1]
    kcols = keyval_proj.shape[1]
    t_part = target_hidden.shape[1]
    half = V // 2
    vocab_width = draft_head.shape[1]
    gain_width = width // V
    local_heads = qcols // HEAD_DIM
    swidth = max(1, local_heads // (HEADS // KV_HEADS)) * HEAD_DIM
    assert V == R and V % 2 == 0 and output_proj.shape == (qcols, part)
    assert kcols // swidth in (1, 2)
    vm = pl.BlockSpec(memory_space=pltpu.VMEM)
    hbm = pl.BlockSpec(memory_space=pl.ANY)
    buffer = pltpu.VMEM
    outs = pl.pallas_call(
        functools.partial(step_kernel, V, R),
        out_shape=(
            jax.ShapeDtypeStruct((1, 1), f32),
            jax.ShapeDtypeStruct(draft_head.shape, bf16),
            jax.ShapeDtypeStruct((1, gain_width), f32),
            jax.ShapeDtypeStruct(output_proj.shape, bf16),
            jax.ShapeDtypeStruct(query_proj.shape, bf16),
            jax.ShapeDtypeStruct((R, rows, part), bf16),
            jax.ShapeDtypeStruct((R, rows, kcols), bf16),
        ),
        in_specs=[vm, vm, hbm, vm, vm, hbm, hbm, hbm, vm, hbm, vm, vm, vm],
        out_specs=(vm, hbm, vm, hbm, hbm, vm, vm),
        scratch_shapes=[
            buffer(target_head.shape, bf16),
            buffer(query_proj.shape, bf16),
            buffer(keyval_proj.shape, bf16),
            buffer((2, *draft_head.shape), bf16),
            buffer((V, *output_proj.shape), bf16),
            buffer(draft_head.shape, bf16),
            buffer(output_proj.shape, bf16),
            buffer(query_proj.shape, bf16),
            buffer((1, t_part * V), f32),
            buffer((R, rows, t_part), bf16),
            buffer((V, R, rows, t_part), bf16),
            buffer((R, rows, part), bf16),
            buffer((rows, part), bf16),
            buffer((R, rows, part), bf16),
            buffer((R, rows, part), bf16),
            buffer((kcols // swidth, R, rows, swidth), f32),
            buffer((2, R, rows, swidth), f32),
            buffer((R, rows, qcols), f32),
            buffer((R, rows, qcols), f32),
            buffer((R, rows, qcols), bf16),
            buffer((V, rows, qcols), bf16),
            buffer((R, rows, part), f32),
            buffer((R, rows, part), f32),
            buffer((R, 1, part), f32),
            buffer((2, half, rows, width), bf16),
            buffer((half, rows, 2 * vocab_width), f32),
            buffer((R, rows, vocab_width), f32),
            buffer((2, half, rows, vocab_width), f32),
            buffer((half * R, 8, half * rows), f32),
            buffer((2, 8, 128), f32),
            buffer((2, half * rows, vocab_width), bf16),
            buffer((2, half * rows, vocab_width), bf16),
            buffer((half, rows, width), f32),
            buffer((half, rows, width), f32),
            buffer((R, rows, part + 128), f32),
            buffer((R, rows, part + 128), f32),
            buffer((V, rows, part), bf16),
            buffer((V, rows, qcols), f32),
            buffer((R, rows, qcols), f32),
            buffer((8, part), f32),
            buffer((V, 8, part), f32),
            buffer((2, rows, swidth), f32 if swidth == kcols else bf16),
            buffer((R, 2, rows, swidth), f32 if swidth == kcols else bf16),
            buffer((R, rows, qcols), bf16),
            pltpu.SemaphoreType.DMA((9,)),
            pltpu.SemaphoreType.DMA((16 * R + 6 * V + half * R + 16,)),
            pltpu.SemaphoreType.DMA((6 * R + 6 * V + 16,)),
            pltpu.SemaphoreType.DMA((2, R)),
            pltpu.SemaphoreType.DMA((V,)),
            pltpu.SemaphoreType.DMA((R,)),
            pltpu.SemaphoreType.DMA((V,)),
            pltpu.SemaphoreType.DMA((R, 2)),
            pltpu.SemaphoreType.DMA((half * R,)),
        ],
        compiler_params=pltpu.CompilerParams(
            collective_id=0, has_side_effects=True, vmem_limit_bytes=56 << 20
        ),
        name="distill_step",
    )(
        target_hidden,
        target_gain.reshape(-1, 128),
        target_head,
        draft_input,
        attn_gain.reshape(-1, 128),
        query_proj,
        keyval_proj,
        output_proj,
        draft_gain.reshape(-1, 128),
        draft_head,
        parents.reshape(1, -1),
        token_ids.reshape(1, -1),
        valid_counts.reshape(1, -1),
    )
    loss, head, gain, query, keyval, output = pl.pallas_call(
        functools.partial(finish_kernel, R),
        out_shape=(
            jax.ShapeDtypeStruct((1, 1), f32),
            jax.ShapeDtypeStruct(draft_head.shape, bf16),
            jax.ShapeDtypeStruct((1, gain_width), f32),
            jax.ShapeDtypeStruct(query_proj.shape, bf16),
            jax.ShapeDtypeStruct(keyval_proj.shape, bf16),
            jax.ShapeDtypeStruct(output_proj.shape, bf16),
        ),
        in_specs=[vm, hbm, vm, hbm, hbm, vm, vm],
        out_specs=(vm, hbm, vm, hbm, vm, hbm),
        scratch_shapes=[
            buffer(draft_head.shape, bf16),
            buffer(output_proj.shape, bf16),
            buffer(query_proj.shape, bf16),
            pltpu.SemaphoreType.DMA((6,)),
        ],
        name="distill_finish",
    )(*outs)
    return loss.reshape(1), head, gain.reshape(-1), query, keyval, output


def solution(mesh):
    in_specs = (
        P(("job", "req"), "vocab"),
        P("job"),
        P("job", ("vocab", "req")),
        P(("job", "req"), None),
        P("job"),
        P(("job", "req"), "vocab"),
        P(("job", "req"), "vocab"),
        P(("job", "vocab"), "req"),
        P("job"),
        P("job", ("vocab", "req")),
        P(("job", "req")),
        P("job"),
        P("job"),
    )
    out_specs = (
        P("job"),
        P("job", ("vocab", "req")),
        P(("job", "vocab")),
        P(("job", "req"), "vocab"),
        P(("job", "req"), "vocab"),
        P(("job", "vocab"), "req"),
    )
    return jax.shard_map(
        functools.partial(shards, mesh.shape["vocab"], mesh.shape["req"]),
        mesh=mesh,
        in_specs=in_specs,
        out_specs=out_specs,
        check_vma=False,
    )
```

```python
import functools
import math

import jax
import jax.numpy as jnp
from jax import lax
from jax.experimental import pallas as pl
from jax.experimental.pallas import tpu as pltpu
from jax.sharding import PartitionSpec as P

HEADS = 32
KV_HEADS = 8
HEAD_DIM = 64

epsilon = 1e-05
rope_base = 500000.0
hard_weight = 0.5
loss_scale = 1024.0
f32 = jnp.float32
bf16 = jnp.bfloat16
MESH = pl.DeviceIdType.MESH


def dot_nn(a, b):
    return jnp.dot(a, b, preferred_element_type=f32)


def dot_tn(a, b):
    return lax.dot_general(a, b, (((0,), (0,)), ((), ())), preferred_element_type=f32)


def dot_nt(a, b):
    return lax.dot_general(a, b, (((1,), (1,)), ((), ())), preferred_element_type=f32)


def as_row(ref, first, count):
    lanes = ref.shape[1]
    values = ref[...].astype(f32)
    rows = range(first // lanes, (first + count) // lanes)
    return jnp.concatenate([values[k : k + 1] for k in rows], axis=1)


def grouped(lhs, rhs, out, groups, step):
    for first in range(0, out.shape[0], step):
        value = None
        for g in range(groups):
            term = dot_tn(lhs(g, first, step), rhs(g)).astype(bf16).astype(f32)
            value = term if value is None else value + term
        out[first : first + step] = value.astype(bf16)


def total(ref, count):
    value = ref[0]
    for k in range(1, count):
        value = value + ref[k]
    return value


def swap_halves(values):
    width = values.shape[1]
    half = HEAD_DIM // 2
    lane = lax.broadcasted_iota(jnp.int32, values.shape, 1)
    if width % 128 == 0:
        ahead = pltpu.roll(values, width - half, 1)
        behind = pltpu.roll(values, half, 1)
        return jnp.where(lane % HEAD_DIM < half, -ahead, behind)
    pieces = []
    for head in range(width // HEAD_DIM):
        lead = values[:, head * HEAD_DIM : head * HEAD_DIM + half]
        trail = values[:, head * HEAD_DIM + half : (head + 1) * HEAD_DIM]
        pieces += [-trail, lead]
    return jnp.concatenate(pieces, axis=1)


def angles(depth, rows, width):
    lane = lax.broadcasted_iota(jnp.int32, (rows, width), 1) % (HEAD_DIM // 2)
    frequency = jnp.exp(lane.astype(f32) * (-2.0 / HEAD_DIM * math.log(rope_base)))
    return depth * frequency


def group_of(v, V):
    return v // 2 * (1 - v % 2) + (V - 1 - v // 2) * (v % 2)


def owner_of(group, V):
    upper = group // (V // 2)
    return 2 * group * (1 - upper) + (2 * (V - 1 - group) + 1) * upper


def step_kernel(
    V,
    R,
    target_hidden_hbm,
    target_gain_hbm,
    target_head,
    draft_input_hbm,
    attn_gain_hbm,
    query_proj,
    keyval_proj,
    output_proj,
    draft_gain_hbm,
    draft_head,
    parents_hbm,
    token_ids_hbm,
    valid_counts_hbm,
    mean_loss,
    grad_head,
    grad_gain,
    grad_output,
    x_rows,
    query_rows,
    keyval_rows,
    target_hidden,
    target_gain,
    draft_input,
    attn_gain,
    draft_gain,
    parents,
    token_ids,
    valid_counts,
    w_target,
    w_query,
    w_keyval,
    wd,
    wo,
    head_block,
    output_block,
    t_gain,
    t1,
    t2,
    d_out,
    d_in,
    x_out,
    x_in,
    k_out,
    k_in,
    a_out,
    a_in,
    mix,
    hm,
    hid,
    hnorm,
    gains,
    nd,
    dl,
    tl_out,
    tl_in,
    stat_all,
    loss_all,
    lb_out,
    lb_in,
    b_out,
    b_in,
    c_out,
    c_in,
    inner_all,
    ob,
    m_out,
    m_in,
    gain_out,
    gain_in,
    kv_out,
    kv_in,
    qg,
    local_sems,
    send_sems,
    recv_sems,
    k_sems,
    hm_sems,
    m_sems,
    gain_sems,
    kv_sems,
    stat_sems,
    c_sems,
):
    v = lax.axis_index("vocab")
    r = lax.axis_index("req")
    half = V // 2
    chip, core = v // 2, lax.rem(v, 2)
    sibling = v + 1 - 2 * core
    group = group_of(v, V)
    rows, width = draft_input.shape
    all_rows = rows * R
    n = rows * half
    part = width // R
    qcols = query_proj.shape[1]
    kcols = keyval_proj.shape[1]
    vocab_width = draft_head.shape[1]
    t_part = target_hidden.shape[1]
    t_width = t_part * V
    local_heads = qcols // HEAD_DIM
    head_group = HEADS // KV_HEADS
    shared = max(1, local_heads // head_group)
    spread = local_heads // shared
    swidth = shared * HEAD_DIM
    pieces = kcols // swidth
    inv_root = HEAD_DIM ** (-0.5)

    loads = []
    for index, (source, target) in enumerate(
        (
            (draft_input_hbm, draft_input),
            (attn_gain_hbm, attn_gain),
            (query_proj, w_query),
            (keyval_proj, w_keyval),
            (target_head, w_target),
            (output_proj, wo.at[v]),
            (draft_head, wd.at[core]),
            (parents_hbm, parents),
            (target_hidden_hbm, target_hidden),
            (target_gain_hbm, target_gain),
            (draft_gain_hbm, draft_gain),
            (token_ids_hbm, token_ids),
            (valid_counts_hbm, valid_counts),
        )
    ):
        load = pltpu.make_async_copy(source, target, local_sems.at[index])
        load.start()
        loads.append(load)

    def wait_load(index):
        loads[index].wait()

    barrier = pltpu.get_barrier_semaphore()
    for dv in range(V):
        for dr in range(R):
            if dv or dr:
                pl.semaphore_signal(
                    barrier,
                    inc=1,
                    device_id={"vocab": lax.rem(v + dv, V), "req": lax.rem(r + dr, R)},
                    device_id_type=MESH,
                )

    sent, sent_unless = [], []
    used = [0, 0]

    def describe(source, target, device, recv):
        used[0] += 1
        return pltpu.make_async_remote_copy(
            src_ref=source,
            dst_ref=target,
            send_sem=send_sems.at[used[0] - 1],
            recv_sem=recv,
            device_id=device,
            device_id_type=MESH,
        )

    def push(source, target, device, recv=None):
        if recv is None:
            recv = recv_sems.at[used[1]]
            used[1] += 1
        copy = describe(source, target, device, recv)
        copy.start()
        sent.append(copy)
        return copy

    def push_unless(here, source, target, device, recv):
        copy = describe(source, target, device, recv)

        @pl.when(jnp.logical_not(here))
        def _():
            copy.start()

        @pl.when(here)
        def _():
            pltpu.make_async_copy(source, target, recv).start()

        sent_unless.append((copy, here))

    def landed(target, recv):
        pltpu.make_async_remote_copy(
            src_ref=target,
            dst_ref=target,
            send_sem=recv,
            recv_sem=recv,
            device_id={"vocab": sibling},
            device_id_type=MESH,
        ).wait_recv()

    def over_req(source, target):
        peers = [lax.rem(r + k, R) for k in range(1, R)]
        return [push(source(p), target.at[r], {"req": p}) for p in peers]

    def over_chips(source, target):
        chips = [lax.rem(chip + k, half) for k in range(1, half)]
        return [push(source(c), target, {"vocab": 2 * c + core}) for c in chips]

    def arrive(copies):
        for copy in copies:
            copy.wait_recv()

    wait_load(0)
    wait_load(1)
    inputs = draft_input[...].astype(f32)
    scale = lax.rsqrt(jnp.mean(inputs * inputs, axis=-1, keepdims=True) + epsilon)
    normed = (inputs * scale * as_row(attn_gain, 0, width)).astype(bf16)
    for p in range(R):
        x_out[p] = normed[:, p * part : (p + 1) * part]
    x_in[r] = x_out[r]

    pl.semaphore_wait(barrier, V * R - 1)
    got_x = over_req(lambda p: x_out.at[p], x_in)
    wait_load(8)
    t1[r] = target_hidden[...]
    got_t1 = over_req(lambda p: t1.at[r], t1)
    early = qcols * 3 // 8

    def wo_block(slot, first, last):
        return wo.at[slot, pl.ds(first, last - first)]

    got_wo = over_chips(
        lambda c: output_proj.at[:early], wo_block(v, 0, early)
    )
    got_wd = push(draft_head, wd.at[core], {"vocab": sibling})
    for p in range(R):
        d_out[p] = draft_input[:, p * part : (p + 1) * part]
    here = r == group
    for k in range(1, R):
        p = lax.rem(r + k, R)
        copy = describe(d_out.at[p], d_in, {"req": p}, local_sems.at[16])

        @pl.when(here)
        def _():
            copy.start()

        sent_unless.append((copy, jnp.logical_not(here)))

    @pl.when(here)
    def _():
        d_in[...] = d_out[r]

    def d_landed():
        @pl.when(r != group)
        def _():
            landed(d_in, local_sems.at[16])

    wait_load(7)
    row_i = lax.broadcasted_iota(jnp.int32, (rows, rows), 0)
    col_i = lax.broadcasted_iota(jnp.int32, (rows, rows), 1)
    eye = row_i == col_i
    parent_col = jnp.sum(
        jnp.where(eye, parents[...].astype(f32), 0.0), axis=1, keepdims=True
    )
    linked = jnp.where(
        jnp.logical_or(eye, parent_col == col_i.astype(f32)), 1.0, 0.0
    ).astype(f32)
    for doubling in range(max(1, (rows - 1).bit_length())):
        half_linked = linked.astype(bf16)
        linked = jnp.minimum(dot_nn(half_linked, half_linked), 1.0)
    depth = jnp.sum(linked, axis=1, keepdims=True) - 1.0
    table = min(qcols, 128)
    angle = angles(depth, rows, table)
    q_cos = jnp.concatenate([jnp.cos(angle)] * (qcols // table), axis=1)
    q_sin = jnp.concatenate([jnp.sin(angle)] * (qcols // table), axis=1)
    s_cos, s_sin = q_cos[:, :swidth], q_sin[:, :swidth]

    wait_load(3)
    arrive(got_x)
    x_all = x_in[...].reshape(all_rows, part)
    kv_part = dot_nn(x_all, w_keyval[...])
    for piece in range(pieces):
        k_out[piece] = kv_part[:, piece * swidth : (piece + 1) * swidth].reshape(
            R, rows, swidth
        )
    kind = v // half
    for k in range(R):
        p = lax.rem(r + k, R)
        for d in range(2):
            target_v = lax.rem(v, half) * 2 + d
            push_unless(
                jnp.logical_and(target_v == v, p == r),
                k_out.at[d * pieces // 2, p],
                k_in.at[kind, r],
                {"vocab": target_v, "req": p},
                k_sems.at[kind, r],
            )

    def k_landed():
        for p in range(R):
            for which in range(2):
                landed(k_in.at[which, p], k_sems.at[which, p])

    wait_load(2)
    a_out[...] = dot_nn(x_all, w_query[...]).reshape(R, rows, qcols)
    got_a = over_req(lambda p: a_out.at[p], a_in)
    a_in[r] = a_out[r]
    got_wo_late = over_chips(
        lambda c: output_proj.at[early:], wo_block(v, early, qcols)
    )
    got_wo_near = push(output_proj, wo.at[v], {"vocab": sibling})
    x_rows[...] = x_in[...]

    wait_load(10)
    wait_load(9)
    wait_load(11)
    wait_load(12)
    for p in range(R):
        gains[p] = as_row(draft_gain, p * part, part)
    t_gain[...] = as_row(target_gain, 0, t_width)

    big_row = lax.broadcasted_iota(jnp.int32, (n, n), 0)
    big_col = lax.broadcasted_iota(jnp.int32, (n, n), 1)
    diagonal = big_row == big_col

    def to_col(row):
        return jnp.sum(jnp.where(diagonal, row, 0.0), axis=1, keepdims=True)

    def to_row(col):
        return jnp.sum(jnp.where(diagonal, col, 0.0), axis=0, keepdims=True)

    def groups_of(index):
        place = index // rows
        return place * (1 - core) + (V - 1 - place) * core

    token_row = lax.broadcasted_iota(jnp.int32, (n, all_rows), 0)
    token_at = lax.broadcasted_iota(jnp.int32, (n, all_rows), 1)
    token_col = jnp.sum(
        jnp.where(
            groups_of(token_row) * rows + token_row % rows == token_at,
            token_ids[...].astype(f32),
            0.0,
        ),
        axis=1,
        keepdims=True,
    )
    lane = lax.broadcasted_iota(jnp.int32, (n, 2 * vocab_width), 1)
    lane_block = lane // vocab_width
    columns = ((2 * chip + lane_block) * R + r) * vocab_width + lane % vocab_width
    onehot = token_col == columns.astype(f32)
    counts = valid_counts[...].astype(f32)
    group_row = lax.broadcasted_iota(jnp.int32, (n, R), 0)
    group_col = lax.broadcasted_iota(jnp.int32, (n, R), 1)
    count_col = jnp.sum(
        jnp.where(groups_of(group_row) == group_col, counts, 0.0), axis=1, keepdims=True
    )
    local_row = (lax.broadcasted_iota(jnp.int32, (n, 1), 0) % rows).astype(f32)
    valid = jnp.where(local_row < count_col, 1.0, 0.0)
    valid_row = to_row(valid)
    valid_total = jnp.sum(counts, axis=1, keepdims=True)

    k_landed()
    key_raw = total(k_in.at[0], R)
    key_rows = (key_raw * s_cos + swap_halves(key_raw) * s_sin).astype(bf16)
    value_rows = total(k_in.at[1], R).astype(bf16)
    arrive(got_a)
    query_raw = total(a_in, R)
    queries = (query_raw * q_cos + swap_halves(query_raw) * q_sin).astype(bf16)

    def stack_heads(values, group):
        return jnp.concatenate(
            [
                values[:, (group * spread + h) * HEAD_DIM : (group * spread + h + 1) * HEAD_DIM]
                for h in range(spread)
            ],
            axis=0,
        )

    def unstack_heads(stacks):
        return jnp.concatenate(
            [stack[h * rows : (h + 1) * rows] for stack in stacks for h in range(spread)],
            axis=1,
        )

    query_stacks = [stack_heads(queries, s) for s in range(shared)]
    allowed = jnp.concatenate([linked] * spread, axis=0) > 0.5
    probs, weights, keys, values, mixes = [], [], [], [], []
    for s in range(shared):
        key = key_rows[:, s * HEAD_DIM : (s + 1) * HEAD_DIM]
        value = value_rows[:, s * HEAD_DIM : (s + 1) * HEAD_DIM]
        scores = dot_nt(query_stacks[s], key) * inv_root
        scores = jnp.where(allowed, scores, -jnp.inf)
        powers = jnp.exp(scores - jnp.max(scores, axis=-1, keepdims=True))
        prob = powers / jnp.sum(powers, axis=-1, keepdims=True)
        weight = prob.astype(bf16)
        probs.append(prob)
        weights.append(weight)
        keys.append(key)
        values.append(value)
        mixes.append(dot_nn(weight, value))
    mix[r] = unstack_heads(mixes).astype(bf16)
    owner = owner_of(r, V)
    for k in range(R):
        p = lax.rem(r + k, R)
        push_unless(
            jnp.logical_and(owner == v, p == r),
            mix.at[r],
            hm.at[v],
            {"vocab": owner, "req": p},
            hm_sems.at[v],
        )

    def hm_landed():
        for p in range(V):
            landed(hm.at[p], hm_sems.at[p])

    got_wo_pass = []
    for copies, low, high in ((got_wo, 0, early), (got_wo_late, early, qcols)):
        arrive(copies)
        for k in range(1, half):
            sender = lax.rem(v + V - 2 * k, V)
            got_wo_pass.append(
                push(wo_block(sender, low, high), wo_block(sender, low, high), {"vocab": sibling})
            )
    arrive(got_t1)
    t2[v] = t1[...]
    got_t2_far = over_chips(lambda c: t2.at[v], t2.at[v])
    got_t2_near = push(t2.at[v], t2.at[v], {"vocab": sibling})
    got_mix = over_req(lambda p: mix.at[r], mix)

    wait_load(5)
    got_wo_near.wait_recv()
    d_landed()
    value = d_in[...].astype(f32)
    hm_landed()
    arrive(got_wo_pass)
    attn_out = None
    for p in range(V):
        term = dot_nn(hm[p], wo[p])
        attn_out = term if attn_out is None else attn_out + term
    hid[r] = value + attn_out
    got_h = over_req(lambda p: hid.at[r], hid)

    arrive(got_t2_far)
    got_pass = []
    for k in range(1, half):
        sender = lax.rem(v + V - 2 * k, V)
        got_pass.append(push(t2.at[sender], t2.at[sender], {"vocab": sibling}))
    wait_load(4)
    got_t2_near.wait_recv()
    arrive(got_pass)
    squares = jnp.zeros((all_rows, 1), f32)
    for p in range(V):
        piece = t2[p].reshape(all_rows, t_part).astype(f32)
        squares = squares + jnp.sum(piece * piece, axis=-1, keepdims=True)
    t_scale = lax.rsqrt(squares / t_width + epsilon)

    def target_part(first, last):
        value = None
        for p in range(first, last):
            piece = t2[p].reshape(all_rows, t_part).astype(f32)
            piece = (piece * t_scale * t_gain[:, p * t_part : (p + 1) * t_part]).astype(bf16)
            term = dot_nn(piece, w_target[p * t_part : (p + 1) * t_part])
            value = term if value is None else value + term
        return value

    first_logits = target_part(0, half)

    arrive(got_h)
    squares = jnp.zeros((rows, 1), f32)
    for p in range(R):
        squares = squares + jnp.sum(hid[p] * hid[p], axis=-1, keepdims=True)
    hidden_scale = lax.rsqrt(squares / width + epsilon)
    for p in range(R):
        norm = hid[p] * hidden_scale
        hnorm[p] = norm
        nd[core, chip, :, p * part : (p + 1) * part] = (norm * gains[p]).astype(bf16)
    got_nd = over_chips(lambda c: nd.at[core, chip], nd.at[core, chip])
    tl_out[...] = (first_logits + target_part(half, V)).reshape(R, rows, vocab_width)
    got_tl = []
    for k in range(half):
        mine = k * (1 - core) + (V - 1 - k) * core
        other = k * core + (V - 1 - k) * (1 - core)
        got_tl.append(push(tl_out.at[other], tl_in.at[core, k], {"vocab": sibling}))
        tl_in[core, k] = tl_out[mine]
    wait_load(6)
    got_wd.wait_recv()

    def draft_part(place):
        for b in range(2):
            dl[place, :, b * vocab_width : (b + 1) * vocab_width] = dot_nn(
                nd[core, place], wd[b]
            )

    draft_part(chip)
    arrive(got_tl)
    target_logits = jnp.concatenate(
        [tl_in[b].reshape(n, vocab_width) for b in range(2)], axis=1
    )
    t_max = jnp.max(target_logits, axis=1, keepdims=True)
    t_pow = jnp.exp(target_logits - t_max)
    t_sum = jnp.sum(t_pow, axis=1, keepdims=True)
    arrive(got_nd)
    for k in range(1, half):
        draft_part(lax.rem(chip + k, half))

    draft_logits = dl[...].reshape(n, 2 * vocab_width)
    d_max = jnp.max(draft_logits, axis=1, keepdims=True)
    d_pow = jnp.exp(draft_logits - d_max)
    stats = (
        t_max,
        d_max,
        t_sum,
        jnp.sum(t_pow * (target_logits - draft_logits), axis=1, keepdims=True),
        jnp.sum(d_pow, axis=1, keepdims=True),
        jnp.sum(jnp.where(onehot, draft_logits, 0.0), axis=1, keepdims=True),
    )
    stats = [to_row(item) for item in stats]
    stat_kind = lax.broadcasted_iota(jnp.int32, (8, n), 0)

    def pack(items):
        packed = jnp.zeros((8, n), f32)
        for index, item in enumerate(items):
            packed = jnp.where(stat_kind == index, item, packed)
        return packed

    def combine(ref, count):
        top = ref[0]
        for k in range(1, count):
            top = jnp.maximum(top, ref[k])
        t_top, d_top = top[0:1], top[1:2]
        t_sum, cross, d_sum, token = 0.0, 0.0, 0.0, 0.0
        for k in range(count):
            piece = ref[k]
            t_factor = jnp.exp(piece[0:1] - t_top)
            t_sum = t_sum + piece[2:3] * t_factor
            cross = cross + piece[3:4] * t_factor
            d_sum = d_sum + piece[4:5] * jnp.exp(piece[1:2] - d_top)
            token = token + piece[5:6]
        return t_top, d_top, t_sum, cross, d_sum, token

    place = chip * R + r
    stat_all[place] = pack(stats)
    got_stats = []
    for dc in range(half):
        for dr in range(R):
            if dc or dr:
                device = {
                    "vocab": 2 * lax.rem(chip + dc, half) + core,
                    "req": lax.rem(r + dr, R),
                }
                got_stats.append(
                    push(
                        stat_all.at[place],
                        stat_all.at[place],
                        device,
                        stat_sems.at[dc * R + dr],
                    )
                )
    got_nd_near = push(nd.at[core], nd.at[core], {"vocab": sibling})
    arrive(got_stats)
    t_top, d_top, target_total, cross_total, draft_total, token_logit = combine(
        stat_all, half * R
    )

    row_coef = loss_scale * valid / valid_total
    target_prob = t_pow * to_col(jnp.exp(stats[0] - t_top) / target_total)
    draft_prob = d_pow * to_col(jnp.exp(stats[1] - d_top) / draft_total)
    logit_back = (
        row_coef
        * (
            (1.0 + hard_weight) * draft_prob
            - target_prob
            - jnp.where(onehot, hard_weight, 0.0)
        )
    ).astype(bf16)

    got_b = []
    for p in range(R):
        row_part = None
        for b in range(2):
            term = dot_nt(
                logit_back[:, b * vocab_width : (b + 1) * vocab_width],
                wd[b, p * part : (p + 1) * part],
            )
            row_part = term if row_part is None else row_part + term
        b_out[p] = row_part.reshape(half, rows, part)
        got_b.append(over_chips(lambda c: b_out.at[p, c], b_in.at[p, chip]))
        b_in[p, chip] = b_out[p, chip]
    for b in range(2):
        lb_out[b] = logit_back[:, b * vocab_width : (b + 1) * vocab_width]
    got_lb = push(lb_out.at[1 - core], lb_in.at[core], {"vocab": sibling})
    lb_in[core] = lb_out[core]
    target_lse = t_top + jnp.log(target_total)
    draft_lse = d_top + jnp.log(draft_total)
    row_loss = (
        cross_total / target_total
        - target_lse
        + draft_lse
        + hard_weight * (draft_lse - token_logit)
    )
    loss_all[core] = jnp.broadcast_to(
        jnp.sum(valid_row * row_loss, axis=1, keepdims=True), (8, 128)
    )
    got_loss = push(loss_all.at[core], loss_all.at[core], {"vocab": sibling})
    got_nd_near.wait_recv()
    got_lb.wait_recv()
    lb_all = lb_in[...].reshape(all_rows, vocab_width)
    for p in range(R):
        head_block[p * part : (p + 1) * part] = dot_tn(
            nd[:, :, :, p * part : (p + 1) * part].reshape(all_rows, part), lb_all
        ).astype(bf16)
    head_store = pltpu.make_async_copy(head_block, grad_head, local_sems.at[13])
    head_store.start()

    inner = jnp.zeros((rows, 1), f32)
    for p in range(R):
        arrive(got_b[p])
        piece = total(b_in.at[p], half)
        c_out[p] = piece
        push_unless(p == r, c_out.at[p], c_in.at[r], {"req": p}, c_sems.at[r])
        inner = inner + jnp.sum(piece * gains[p] * hnorm[p], axis=-1, keepdims=True)
    inner_all[r] = jnp.broadcast_to(inner, (rows, 128))
    got_inner = over_req(lambda p: inner_all.at[r], inner_all)

    def c_landed():
        for p in range(R):
            landed(c_in.at[p], c_sems.at[p])

    got_loss.wait_recv()
    mean_loss[...] = (loss_all[0] + loss_all[1])[0:1, 0:1] / valid_total
    arrive(got_inner)
    inner = total(inner_all, R)[:, :1] / width
    c_landed()
    row_back = total(c_in, R)
    norm = hnorm[r]
    out_back = (hidden_scale * (row_back * gains[r] - norm * inner)).astype(bf16)
    ob[v] = out_back
    for k in range(V):
        p = lax.rem(v + k, V)
        m_out[p] = dot_nt(out_back, wo[p])
        push_unless(
            jnp.logical_and(p == v, group == r),
            m_out.at[p],
            m_in.at[r],
            {"vocab": p, "req": group},
            m_sems.at[r],
        )

    def m_landed():
        for p in range(R):
            landed(m_in.at[p], m_sems.at[p])

    got_ob = [
        push(ob.at[v], ob.at[v], {"vocab": lax.rem(v + k, V)}) for k in range(1, V)
    ]
    gain_out[...] = jnp.sum(row_back * norm, axis=0, keepdims=True)
    for k in range(R):
        p = lax.rem(r + k, R)
        push_unless(
            jnp.logical_and(r == v, p == r),
            gain_out,
            gain_in.at[v],
            {"vocab": r, "req": p},
            gain_sems.at[v],
        )

    def gain_landed():
        for p in range(V):
            landed(gain_in.at[p], gain_sems.at[p])

    m_landed()
    mix_back = total(m_in, R).astype(bf16)
    query_parts, key_parts, value_parts = [], [], []
    for s in range(shared):
        back_stack = stack_heads(mix_back, s)
        prob_back = dot_nt(back_stack, values[s])
        delta = jnp.sum(probs[s] * prob_back, axis=-1, keepdims=True)
        score_back = (probs[s] * (prob_back - delta) * inv_root).astype(bf16)
        query_parts.append(dot_nn(score_back, keys[s]))
        key_parts.append(dot_tn(score_back, query_stacks[s]))
        value_parts.append(dot_tn(weights[s], back_stack))
    key_back = jnp.concatenate(key_parts, axis=1)
    key_back = key_back * s_cos - swap_halves(key_back) * s_sin
    kv_out[0] = key_back.astype(kv_out.dtype)
    kv_out[1] = jnp.concatenate(value_parts, axis=1).astype(kv_out.dtype)
    for k in range(R):
        p = lax.rem(r + k, R)
        for which in range(2):
            target_v = which * half + chip
            push_unless(
                jnp.logical_and(target_v == v, p == r),
                kv_out.at[which],
                kv_in.at[r, core],
                {"vocab": target_v, "req": p},
                kv_sems.at[r, core],
            )

    def kv_landed():
        for p in range(R):
            for d in range(2):
                landed(kv_in.at[p, d], kv_sems.at[p, d])

    query_back = unstack_heads(query_parts)
    qg[r] = (query_back * q_cos - swap_halves(query_back) * q_sin).astype(bf16)
    got_qg = over_req(lambda p: qg.at[r], qg)

    arrive(got_mix)
    arrive(got_ob)
    grouped(
        lambda g, a, count: mix[g, :, a : a + count],
        lambda g: ob[owner_of(g, V)],
        output_block,
        R,
        128,
    )
    output_store = pltpu.make_async_copy(output_block, grad_output, local_sems.at[14])
    output_store.start()

    gain_landed()
    grad_gain[...] = total(gain_in, V)
    arrive(got_qg)
    query_rows[...] = qg[...]
    kv_landed()
    for p in range(R):
        if pieces == 1:
            keyval_rows[p] = (kv_in[p, 0] + kv_in[p, 1]).astype(bf16)
        else:
            for d in range(2):
                keyval_rows[p, :, d * swidth : (d + 1) * swidth] = kv_in[p, d]
    head_store.wait()
    output_store.wait()
    for copy in sent:
        copy.wait_send()
    for copy, here in sent_unless:

        @pl.when(jnp.logical_not(here))
        def _():
            copy.wait_send()


def finish_kernel(
    R,
    loss_in,
    head_in,
    gain_in,
    output_in,
    x_in,
    query_in,
    keyval_in,
    mean_loss,
    grad_head,
    grad_gain,
    grad_query,
    grad_keyval,
    grad_output,
    x_rows,
    query_rows,
    keyval_rows,
    head_block,
    output_block,
    query_block,
    keyval_block,
    loss_block,
    gain_block,
    sems,
):
    moves = (
        (x_in, x_rows, None),
        (query_in, query_rows, None),
        (keyval_in, keyval_rows, None),
        (head_in, head_block, grad_head),
        (output_in, output_block, grad_output),
        (loss_in, loss_block, mean_loss),
        (gain_in, gain_block, grad_gain),
        (None, query_block, grad_query),
        (None, keyval_block, grad_keyval),
    )
    loads, stores = [], []
    for k, (source, block, target) in enumerate(moves):
        if source is not None:
            loads.append(pltpu.make_async_copy(source, block, sems.at[0, k]))
            loads[-1].start()
        if target is not None:
            stores.append(pltpu.make_async_copy(block, target, sems.at[1, k]))
    loads[0].wait()
    loads[1].wait()
    grouped(lambda g, a, n: x_rows[g, :, a : a + n], lambda g: query_rows[g], query_block, R, 128)
    stores[4].start()
    for k in range(4):
        loads[3 + k].wait()
        stores[k].start()
    loads[2].wait()
    grouped(lambda g, a, n: x_rows[g, :, a : a + n], lambda g: keyval_rows[g], keyval_block, R, 128)
    stores[5].start()
    for store in stores:
        store.wait()


def shards(
    V,
    R,
    target_hidden,
    target_gain,
    target_head,
    draft_input,
    attn_gain,
    query_proj,
    keyval_proj,
    output_proj,
    draft_gain,
    draft_head,
    parents,
    token_ids,
    valid_counts,
):
    rows, width = draft_input.shape
    part = width // R
    qcols = query_proj.shape[1]
    kcols = keyval_proj.shape[1]
    t_part = target_hidden.shape[1]
    half = V // 2
    vocab_width = draft_head.shape[1]
    gain_width = width // V
    local_heads = qcols // HEAD_DIM
    swidth = max(1, local_heads // (HEADS // KV_HEADS)) * HEAD_DIM
    assert V == R and V % 2 == 0 and output_proj.shape == (qcols, part)
    assert kcols // swidth in (1, 2)
    vm = pl.BlockSpec(memory_space=pltpu.VMEM)
    hbm = pl.BlockSpec(memory_space=pl.ANY)
    buffer = pltpu.VMEM
    outs = pl.pallas_call(
        functools.partial(step_kernel, V, R),
        out_shape=(
            jax.ShapeDtypeStruct((1, 1), f32),
            jax.ShapeDtypeStruct(draft_head.shape, bf16),
            jax.ShapeDtypeStruct((1, gain_width), f32),
            jax.ShapeDtypeStruct(output_proj.shape, bf16),
            jax.ShapeDtypeStruct((R, rows, part), bf16),
            jax.ShapeDtypeStruct((R, rows, qcols), bf16),
            jax.ShapeDtypeStruct((R, rows, kcols), bf16),
        ),
        in_specs=[hbm] * 13,
        out_specs=(vm, hbm, vm, hbm, vm, vm, vm),
        scratch_shapes=[
            buffer(target_hidden.shape, bf16),
            buffer((t_part * V // 128, 128), bf16),
            buffer(draft_input.shape, bf16),
            buffer((width // 128, 128), bf16),
            buffer((width // 128, 128), bf16),
            buffer((1, parents.shape[0]), jnp.int32),
            buffer((1, token_ids.shape[0]), jnp.int32),
            buffer((1, valid_counts.shape[0]), jnp.int32),
            buffer(target_head.shape, bf16),
            buffer(query_proj.shape, bf16),
            buffer(keyval_proj.shape, bf16),
            buffer((2, *draft_head.shape), bf16),
            buffer((V, *output_proj.shape), bf16),
            buffer(draft_head.shape, bf16),
            buffer(output_proj.shape, bf16),
            buffer((1, t_part * V), f32),
            buffer((R, rows, t_part), bf16),
            buffer((V, R, rows, t_part), bf16),
            buffer((R, rows, part), bf16),
            buffer((rows, part), bf16),
            buffer((R, rows, part), bf16),
            buffer((R, rows, part), bf16),
            buffer((kcols // swidth, R, rows, swidth), f32),
            buffer((2, R, rows, swidth), f32),
            buffer((R, rows, qcols), f32),
            buffer((R, rows, qcols), f32),
            buffer((R, rows, qcols), bf16),
            buffer((V, rows, qcols), bf16),
            buffer((R, rows, part), f32),
            buffer((R, rows, part), f32),
            buffer((R, 1, part), f32),
            buffer((2, half, rows, width), bf16),
            buffer((half, rows, 2 * vocab_width), f32),
            buffer((R, rows, vocab_width), f32),
            buffer((2, half, rows, vocab_width), f32),
            buffer((half * R, 8, half * rows), f32),
            buffer((2, 8, 128), f32),
            buffer((2, half * rows, vocab_width), bf16),
            buffer((2, half * rows, vocab_width), bf16),
            buffer((R, half, rows, part), f32),
            buffer((R, half, rows, part), f32),
            buffer((R, rows, part), f32),
            buffer((R, rows, part), f32),
            buffer((R, rows, 128), f32),
            buffer((V, rows, part), bf16),
            buffer((V, rows, qcols), f32),
            buffer((R, rows, qcols), f32),
            buffer((1, part), f32),
            buffer((V, 1, part), f32),
            buffer((2, rows, swidth), f32 if swidth == kcols else bf16),
            buffer((R, 2, rows, swidth), f32 if swidth == kcols else bf16),
            buffer((R, rows, qcols), bf16),
            pltpu.SemaphoreType.DMA((17,)),
            pltpu.SemaphoreType.DMA((20 * R + 8 * V + 2 * half * R + 16,)),
            pltpu.SemaphoreType.DMA((8 * R + 8 * V + half * R + 16,)),
            pltpu.SemaphoreType.DMA((2, R)),
            pltpu.SemaphoreType.DMA((V,)),
            pltpu.SemaphoreType.DMA((R,)),
            pltpu.SemaphoreType.DMA((V,)),
            pltpu.SemaphoreType.DMA((R, 2)),
            pltpu.SemaphoreType.DMA((half * R,)),
            pltpu.SemaphoreType.DMA((R,)),
        ],
        compiler_params=pltpu.CompilerParams(
            collective_id=0, has_side_effects=True, vmem_limit_bytes=56 << 20
        ),
        name="distill_step",
    )(
        target_hidden,
        target_gain.reshape(-1, 128),
        target_head,
        draft_input,
        attn_gain.reshape(-1, 128),
        query_proj,
        keyval_proj,
        output_proj,
        draft_gain.reshape(-1, 128),
        draft_head,
        parents.reshape(1, -1),
        token_ids.reshape(1, -1),
        valid_counts.reshape(1, -1),
    )
    loss, head, gain, query, keyval, output = pl.pallas_call(
        functools.partial(finish_kernel, R),
        out_shape=(
            jax.ShapeDtypeStruct((1, 1), f32),
            jax.ShapeDtypeStruct(draft_head.shape, bf16),
            jax.ShapeDtypeStruct((1, gain_width), f32),
            jax.ShapeDtypeStruct(query_proj.shape, bf16),
            jax.ShapeDtypeStruct(keyval_proj.shape, bf16),
            jax.ShapeDtypeStruct(output_proj.shape, bf16),
        ),
        in_specs=[hbm] * 7,
        out_specs=(hbm,) * 6,
        scratch_shapes=[
            buffer((R, rows, part), bf16),
            buffer((R, rows, qcols), bf16),
            buffer((R, rows, kcols), bf16),
            buffer(draft_head.shape, bf16),
            buffer(output_proj.shape, bf16),
            buffer(query_proj.shape, bf16),
            buffer(keyval_proj.shape, bf16),
            buffer((1, 1), f32),
            buffer((1, gain_width), f32),
            pltpu.SemaphoreType.DMA((2, 9)),
        ],
        name="distill_finish",
    )(*outs)
    return loss.reshape(1), head, gain.reshape(-1), query, keyval, output


def solution(mesh):
    in_specs = (
        P(("job", "req"), "vocab"),
        P("job"),
        P("job", ("vocab", "req")),
        P(("job", "req"), None),
        P("job"),
        P(("job", "req"), "vocab"),
        P(("job", "req"), "vocab"),
        P(("job", "vocab"), "req"),
        P("job"),
        P("job", ("vocab", "req")),
        P(("job", "req")),
        P("job"),
        P("job"),
    )
    out_specs = (
        P("job"),
        P("job", ("vocab", "req")),
        P(("job", "vocab")),
        P(("job", "req"), "vocab"),
        P(("job", "req"), "vocab"),
        P(("job", "vocab"), "req"),
    )
    return jax.shard_map(
        functools.partial(shards, mesh.shape["vocab"], mesh.shape["req"]),
        mesh=mesh,
        in_specs=in_specs,
        out_specs=out_specs,
        check_vma=False,
    )
```

```python
import functools
import math

import jax
import jax.numpy as jnp
from jax import lax
from jax.experimental import pallas as pl
from jax.experimental.pallas import tpu as pltpu
from jax.sharding import PartitionSpec as P

HEADS = 32
KV_HEADS = 8
HEAD_DIM = 64

epsilon = 1e-05
rope_base = 500000.0
hard_weight = 0.5
loss_scale = 1024.0
f32 = jnp.float32
bf16 = jnp.bfloat16
MESH = pl.DeviceIdType.MESH


def dot_nn(a, b):
    return jnp.dot(a, b, preferred_element_type=f32)


def dot_tn(a, b):
    return lax.dot_general(a, b, (((0,), (0,)), ((), ())), preferred_element_type=f32)


def dot_nt(a, b):
    return lax.dot_general(a, b, (((1,), (1,)), ((), ())), preferred_element_type=f32)


def as_row(ref, first, count):
    lanes = ref.shape[1]
    values = ref[...].astype(f32)
    rows = range(first // lanes, (first + count) // lanes)
    return jnp.concatenate([values[k : k + 1] for k in rows], axis=1)


def grouped(lhs, rhs, out, groups, step):
    for first in range(0, out.shape[0], step):
        value = None
        for g in range(groups):
            term = dot_tn(lhs(g, first, step), rhs(g)).astype(bf16).astype(f32)
            value = term if value is None else value + term
        out[first : first + step] = value.astype(bf16)


def total(ref, count):
    value = ref[0]
    for k in range(1, count):
        value = value + ref[k]
    return value


def swap_halves(values):
    width = values.shape[1]
    half = HEAD_DIM // 2
    lane = lax.broadcasted_iota(jnp.int32, values.shape, 1)
    if width % 128 == 0:
        ahead = pltpu.roll(values, width - half, 1)
        behind = pltpu.roll(values, half, 1)
        return jnp.where(lane % HEAD_DIM < half, -ahead, behind)
    pieces = []
    for head in range(width // HEAD_DIM):
        lead = values[:, head * HEAD_DIM : head * HEAD_DIM + half]
        trail = values[:, head * HEAD_DIM + half : (head + 1) * HEAD_DIM]
        pieces += [-trail, lead]
    return jnp.concatenate(pieces, axis=1)


def angles(depth, rows, width):
    lane = lax.broadcasted_iota(jnp.int32, (rows, width), 1) % (HEAD_DIM // 2)
    frequency = jnp.exp(lane.astype(f32) * (-2.0 / HEAD_DIM * math.log(rope_base)))
    return depth * frequency


def group_of(v, V):
    return v // 2 * (1 - v % 2) + (V - 1 - v // 2) * (v % 2)


def owner_of(group, V):
    upper = group // (V // 2)
    return 2 * group * (1 - upper) + (2 * (V - 1 - group) + 1) * upper


def step_kernel(
    V,
    R,
    target_hidden_hbm,
    target_gain_hbm,
    target_head,
    draft_input_hbm,
    attn_gain_hbm,
    query_proj,
    keyval_proj,
    output_proj,
    draft_gain_hbm,
    draft_head,
    parents_hbm,
    token_ids_hbm,
    valid_counts_hbm,
    mean_loss,
    grad_head,
    grad_gain,
    grad_output,
    x_rows,
    query_rows,
    keyval_rows,
    target_hidden,
    target_gain,
    draft_input,
    attn_gain,
    draft_gain,
    parents,
    token_ids,
    valid_counts,
    w_target,
    w_query,
    w_keyval,
    wd,
    wo,
    head_block,
    output_block,
    t_gain,
    t1,
    t2,
    d_out,
    d_in,
    x_out,
    x_in,
    k_out,
    k_in,
    a_out,
    a_in,
    mix,
    hm,
    hid,
    hnorm,
    gains,
    nd,
    dl,
    tl_out,
    tl_in,
    stat_all,
    loss_all,
    lb_out,
    lb_in,
    b_out,
    b_in,
    c_out,
    c_in,
    inner_all,
    ob,
    m_out,
    m_in,
    gain_out,
    gain_in,
    kv_out,
    kv_in,
    qg,
    local_sems,
    send_sems,
    recv_sems,
    k_sems,
    hm_sems,
    m_sems,
    gain_sems,
    kv_sems,
    stat_sems,
    c_sems,
):
    v = lax.axis_index("vocab")
    r = lax.axis_index("req")
    half = V // 2
    chip, core = v // 2, lax.rem(v, 2)
    sibling = v + 1 - 2 * core
    group = group_of(v, V)
    rows, width = draft_input.shape
    all_rows = rows * R
    n = rows * half
    part = width // R
    qcols = query_proj.shape[1]
    kcols = keyval_proj.shape[1]
    vocab_width = draft_head.shape[1]
    t_part = target_hidden.shape[1]
    t_width = t_part * V
    local_heads = qcols // HEAD_DIM
    head_group = HEADS // KV_HEADS
    shared = max(1, local_heads // head_group)
    spread = local_heads // shared
    swidth = shared * HEAD_DIM
    pieces = kcols // swidth
    inv_root = HEAD_DIM ** (-0.5)

    loads = []
    for index, (source, target) in enumerate(
        (
            (draft_input_hbm, draft_input),
            (attn_gain_hbm, attn_gain),
            (query_proj, w_query),
            (keyval_proj, w_keyval),
            (target_head, w_target),
            (output_proj, wo.at[v]),
            (draft_head, wd.at[core]),
            (parents_hbm, parents),
            (target_hidden_hbm, target_hidden),
            (target_gain_hbm, target_gain),
            (draft_gain_hbm, draft_gain),
            (token_ids_hbm, token_ids),
            (valid_counts_hbm, valid_counts),
        )
    ):
        load = pltpu.make_async_copy(source, target, local_sems.at[index])
        load.start()
        loads.append(load)

    def wait_load(index):
        loads[index].wait()

    barrier = pltpu.get_barrier_semaphore()
    for dv in range(V):
        for dr in range(R):
            if dv or dr:
                pl.semaphore_signal(
                    barrier,
                    inc=1,
                    device_id={"vocab": lax.rem(v + dv, V), "req": lax.rem(r + dr, R)},
                    device_id_type=MESH,
                )

    sent, sent_unless = [], []
    used = [0, 0]

    def flush():
        for copy in sent:
            copy.wait_send()
        for copy, here in sent_unless:

            @pl.when(jnp.logical_not(here))
            def _():
                copy.wait_send()

        sent.clear()
        sent_unless.clear()

    def describe(source, target, device, recv):
        used[0] += 1
        return pltpu.make_async_remote_copy(
            src_ref=source,
            dst_ref=target,
            send_sem=send_sems.at[used[0] - 1],
            recv_sem=recv,
            device_id=device,
            device_id_type=MESH,
        )

    def push(source, target, device, recv=None):
        if recv is None:
            recv = recv_sems.at[used[1]]
            used[1] += 1
        copy = describe(source, target, device, recv)
        copy.start()
        sent.append(copy)
        return copy

    def push_unless(here, source, target, device, recv):
        copy = describe(source, target, device, recv)

        @pl.when(jnp.logical_not(here))
        def _():
            copy.start()

        @pl.when(here)
        def _():
            pltpu.make_async_copy(source, target, recv).start()

        sent_unless.append((copy, here))

    def incoming(target, recv):
        return pltpu.make_async_remote_copy(
            src_ref=target,
            dst_ref=target,
            send_sem=recv,
            recv_sem=recv,
            device_id={"vocab": sibling},
            device_id_type=MESH,
        )

    def landed(target, recv):
        incoming(target, recv).wait_recv()

    low = 1 - r // (R // 2)
    far_first = [low * (R - 1 - k) + (1 - low) * k for k in range(R)]
    far_peers = [
        low * (R - 2 - k + (2 * R - 2 - k - r) // R)
        + (1 - low) * (k + 1 - (r - k + R - 1) // R)
        for k in range(R - 1)
    ]

    def over_req(source, target):
        first = used[1]
        used[1] += R
        for k in range(1, R):
            p = lax.rem(r + k, R)
            copy = describe(source(p), target.at[r], {"req": p}, recv_sems.at[first + r])
            copy.start()
            sent.append(copy)
        arrivals = []
        for k in range(1, R):
            p = lax.rem(r + k, R)
            arrivals.append(incoming(target.at[p], recv_sems.at[first + p]))
        return arrivals

    def over_chips(source, target):
        chips = [lax.rem(chip + k, half) for k in range(1, half)]
        return [push(source(c), target, {"vocab": 2 * c + core}) for c in chips]

    def arrive(copies):
        for copy in copies:
            copy.wait_recv()

    wait_load(0)
    wait_load(1)
    inputs = draft_input[...].astype(f32)
    scale = lax.rsqrt(jnp.mean(inputs * inputs, axis=-1, keepdims=True) + epsilon)
    normed = (inputs * scale * as_row(attn_gain, 0, width)).astype(bf16)
    for p in range(R):
        x_out[p] = normed[:, p * part : (p + 1) * part]
    x_in[r] = x_out[r]

    pl.semaphore_wait(barrier, V * R - 1)
    got_x = over_req(lambda p: x_out.at[p], x_in)
    wait_load(8)
    t1[r] = target_hidden[...]
    got_t1 = over_req(lambda p: t1.at[r], t1)
    early = qcols * 3 // 8

    def wo_block(slot, first, last):
        return wo.at[slot, pl.ds(first, last - first)]

    got_wo = over_chips(
        lambda c: output_proj.at[:early], wo_block(v, 0, early)
    )
    got_wd = push(draft_head, wd.at[core], {"vocab": sibling})
    for p in range(R):
        d_out[p] = draft_input[:, p * part : (p + 1) * part]
    here = r == group
    for p in far_peers:
        copy = describe(d_out.at[p], d_in, {"req": p}, local_sems.at[16])

        @pl.when(here)
        def _():
            copy.start()

        sent_unless.append((copy, jnp.logical_not(here)))

    @pl.when(here)
    def _():
        d_in[...] = d_out[r]

    def d_landed():
        @pl.when(r != group)
        def _():
            landed(d_in, local_sems.at[16])

    wait_load(7)
    row_i = lax.broadcasted_iota(jnp.int32, (rows, rows), 0)
    col_i = lax.broadcasted_iota(jnp.int32, (rows, rows), 1)
    eye = row_i == col_i
    parent_col = jnp.sum(
        jnp.where(eye, parents[...].astype(f32), 0.0), axis=1, keepdims=True
    )
    linked = jnp.where(
        jnp.logical_or(eye, parent_col == col_i.astype(f32)), 1.0, 0.0
    ).astype(f32)
    for doubling in range(max(1, (rows - 1).bit_length())):
        half_linked = linked.astype(bf16)
        linked = jnp.minimum(dot_nn(half_linked, half_linked), 1.0)
    depth = jnp.sum(linked, axis=1, keepdims=True) - 1.0
    table = min(qcols, 128)
    angle = angles(depth, rows, table)
    q_cos = jnp.concatenate([jnp.cos(angle)] * (qcols // table), axis=1)
    q_sin = jnp.concatenate([jnp.sin(angle)] * (qcols // table), axis=1)
    s_cos, s_sin = q_cos[:, :swidth], q_sin[:, :swidth]

    wait_load(3)
    arrive(got_x)
    x_all = x_in[...].reshape(all_rows, part)
    kv_part = dot_nn(x_all, w_keyval[...])
    for piece in range(pieces):
        k_out[piece] = kv_part[:, piece * swidth : (piece + 1) * swidth].reshape(
            R, rows, swidth
        )
    kind = v // half
    for p in far_first:
        for d in range(2):
            target_v = lax.rem(v, half) * 2 + d
            push_unless(
                jnp.logical_and(target_v == v, p == r),
                k_out.at[d * pieces // 2, p],
                k_in.at[kind, r],
                {"vocab": target_v, "req": p},
                k_sems.at[kind, r],
            )

    def k_landed():
        for p in range(R):
            for which in range(2):
                landed(k_in.at[which, p], k_sems.at[which, p])

    got_wo_late = over_chips(
        lambda c: output_proj.at[early:], wo_block(v, early, qcols)
    )
    wait_load(2)
    a_out[...] = dot_nn(x_all, w_query[...]).reshape(R, rows, qcols)
    got_a = over_req(lambda p: a_out.at[p], a_in)
    a_in[r] = a_out[r]
    got_wo_near = push(output_proj, wo.at[v], {"vocab": sibling})
    x_rows[...] = x_in[...]

    wait_load(10)
    wait_load(9)
    wait_load(11)
    wait_load(12)
    for p in range(R):
        gains[p] = as_row(draft_gain, p * part, part)
    t_gain[...] = as_row(target_gain, 0, t_width)

    big_row = lax.broadcasted_iota(jnp.int32, (n, n), 0)
    big_col = lax.broadcasted_iota(jnp.int32, (n, n), 1)
    diagonal = big_row == big_col

    def to_col(row):
        return jnp.sum(jnp.where(diagonal, row, 0.0), axis=1, keepdims=True)

    def to_row(col):
        return jnp.sum(jnp.where(diagonal, col, 0.0), axis=0, keepdims=True)

    def groups_of(index):
        place = index // rows
        return place * (1 - core) + (V - 1 - place) * core

    token_row = lax.broadcasted_iota(jnp.int32, (n, all_rows), 0)
    token_at = lax.broadcasted_iota(jnp.int32, (n, all_rows), 1)
    token_col = jnp.sum(
        jnp.where(
            groups_of(token_row) * rows + token_row % rows == token_at,
            token_ids[...].astype(f32),
            0.0,
        ),
        axis=1,
        keepdims=True,
    )
    lane = lax.broadcasted_iota(jnp.int32, (n, 2 * vocab_width), 1)
    lane_block = lane // vocab_width
    columns = ((2 * chip + lane_block) * R + r) * vocab_width + lane % vocab_width
    onehot = token_col == columns.astype(f32)
    counts = valid_counts[...].astype(f32)
    group_row = lax.broadcasted_iota(jnp.int32, (n, R), 0)
    group_col = lax.broadcasted_iota(jnp.int32, (n, R), 1)
    count_col = jnp.sum(
        jnp.where(groups_of(group_row) == group_col, counts, 0.0), axis=1, keepdims=True
    )
    local_row = (lax.broadcasted_iota(jnp.int32, (n, 1), 0) % rows).astype(f32)
    valid = jnp.where(local_row < count_col, 1.0, 0.0)
    valid_row = to_row(valid)
    valid_total = jnp.sum(counts, axis=1, keepdims=True)

    k_landed()
    key_raw = total(k_in.at[0], R)
    key_rows = (key_raw * s_cos + swap_halves(key_raw) * s_sin).astype(bf16)
    value_rows = total(k_in.at[1], R).astype(bf16)
    arrive(got_a)
    query_raw = total(a_in, R)
    queries = (query_raw * q_cos + swap_halves(query_raw) * q_sin).astype(bf16)

    def stack_heads(values, group):
        return jnp.concatenate(
            [
                values[:, (group * spread + h) * HEAD_DIM : (group * spread + h + 1) * HEAD_DIM]
                for h in range(spread)
            ],
            axis=0,
        )

    def unstack_heads(stacks):
        return jnp.concatenate(
            [stack[h * rows : (h + 1) * rows] for stack in stacks for h in range(spread)],
            axis=1,
        )

    query_stacks = [stack_heads(queries, s) for s in range(shared)]
    allowed = jnp.concatenate([linked] * spread, axis=0) > 0.5
    probs, weights, keys, values, mixes = [], [], [], [], []
    for s in range(shared):
        key = key_rows[:, s * HEAD_DIM : (s + 1) * HEAD_DIM]
        value = value_rows[:, s * HEAD_DIM : (s + 1) * HEAD_DIM]
        scores = dot_nt(query_stacks[s], key) * inv_root
        scores = jnp.where(allowed, scores, -jnp.inf)
        powers = jnp.exp(scores - jnp.max(scores, axis=-1, keepdims=True))
        prob = powers / jnp.sum(powers, axis=-1, keepdims=True)
        weight = prob.astype(bf16)
        probs.append(prob)
        weights.append(weight)
        keys.append(key)
        values.append(value)
        mixes.append(dot_nn(weight, value))
    mix[r] = unstack_heads(mixes).astype(bf16)
    owner = owner_of(r, V)
    for p in far_first:
        push_unless(
            jnp.logical_and(owner == v, p == r),
            mix.at[r],
            hm.at[v],
            {"vocab": owner, "req": p},
            hm_sems.at[v],
        )

    def hm_landed():
        for p in range(V):
            landed(hm.at[p], hm_sems.at[p])

    got_wo_pass = []
    for copies, low, high in ((got_wo, 0, early), (got_wo_late, early, qcols)):
        arrive(copies)
        for k in range(1, half):
            sender = lax.rem(v + V - 2 * k, V)
            got_wo_pass.append(
                push(wo_block(sender, low, high), wo_block(sender, low, high), {"vocab": sibling})
            )
    arrive(got_t1)
    t2[v] = t1[...]
    got_t2_far = over_chips(lambda c: t2.at[v], t2.at[v])
    got_t2_near = push(t2.at[v], t2.at[v], {"vocab": sibling})
    got_mix = over_req(lambda p: mix.at[r], mix)

    wait_load(5)
    got_wo_near.wait_recv()
    d_landed()
    value = d_in[...].astype(f32)
    hm_landed()
    arrive(got_wo_pass)
    attn_out = None
    for p in range(V):
        term = dot_nn(hm[p], wo[p])
        attn_out = term if attn_out is None else attn_out + term
    hid[r] = value + attn_out
    got_h = over_req(lambda p: hid.at[r], hid)

    arrive(got_t2_far)
    got_pass = []
    for k in range(1, half):
        sender = lax.rem(v + V - 2 * k, V)
        got_pass.append(push(t2.at[sender], t2.at[sender], {"vocab": sibling}))
    wait_load(4)
    got_t2_near.wait_recv()
    arrive(got_pass)
    squares = jnp.zeros((all_rows, 1), f32)
    for p in range(V):
        piece = t2[p].reshape(all_rows, t_part).astype(f32)
        squares = squares + jnp.sum(piece * piece, axis=-1, keepdims=True)
    t_scale = lax.rsqrt(squares / t_width + epsilon)

    def target_part(first, last):
        value = None
        for p in range(first, last):
            piece = t2[p].reshape(all_rows, t_part).astype(f32)
            piece = (piece * t_scale * t_gain[:, p * t_part : (p + 1) * t_part]).astype(bf16)
            term = dot_nn(piece, w_target[p * t_part : (p + 1) * t_part])
            value = term if value is None else value + term
        return value

    first_logits = target_part(0, half)

    arrive(got_h)
    squares = jnp.zeros((rows, 1), f32)
    for p in range(R):
        squares = squares + jnp.sum(hid[p] * hid[p], axis=-1, keepdims=True)
    hidden_scale = lax.rsqrt(squares / width + epsilon)
    for p in range(R):
        norm = hid[p] * hidden_scale
        hnorm[p] = norm
        nd[core, chip, :, p * part : (p + 1) * part] = (norm * gains[p]).astype(bf16)
    got_nd = over_chips(lambda c: nd.at[core, chip], nd.at[core, chip])
    tl_out[...] = (first_logits + target_part(half, V)).reshape(R, rows, vocab_width)
    got_tl = []
    for k in range(half):
        mine = k * (1 - core) + (V - 1 - k) * core
        other = k * core + (V - 1 - k) * (1 - core)
        got_tl.append(push(tl_out.at[other], tl_in.at[core, k], {"vocab": sibling}))
        tl_in[core, k] = tl_out[mine]
    wait_load(6)
    got_wd.wait_recv()

    def draft_part(place):
        for b in range(2):
            dl[place, :, b * vocab_width : (b + 1) * vocab_width] = dot_nn(
                nd[core, place], wd[b]
            )

    draft_part(chip)
    arrive(got_tl)
    target_logits = jnp.concatenate(
        [tl_in[b].reshape(n, vocab_width) for b in range(2)], axis=1
    )
    t_max = jnp.max(target_logits, axis=1, keepdims=True)
    t_pow = jnp.exp(target_logits - t_max)
    t_sum = jnp.sum(t_pow, axis=1, keepdims=True)
    arrive(got_nd)
    for k in range(1, half):
        draft_part(lax.rem(chip + k, half))

    draft_logits = dl[...].reshape(n, 2 * vocab_width)
    d_max = jnp.max(draft_logits, axis=1, keepdims=True)
    d_pow = jnp.exp(draft_logits - d_max)
    stats = (
        t_max,
        d_max,
        t_sum,
        jnp.sum(t_pow * (target_logits - draft_logits), axis=1, keepdims=True),
        jnp.sum(d_pow, axis=1, keepdims=True),
        jnp.sum(jnp.where(onehot, draft_logits, 0.0), axis=1, keepdims=True),
    )
    stats = [to_row(item) for item in stats]
    stat_kind = lax.broadcasted_iota(jnp.int32, (8, n), 0)

    def pack(items):
        packed = jnp.zeros((8, n), f32)
        for index, item in enumerate(items):
            packed = jnp.where(stat_kind == index, item, packed)
        return packed

    def combine(ref, count):
        top = ref[0]
        for k in range(1, count):
            top = jnp.maximum(top, ref[k])
        t_top, d_top = top[0:1], top[1:2]
        t_sum, cross, d_sum, token = 0.0, 0.0, 0.0, 0.0
        for k in range(count):
            piece = ref[k]
            t_factor = jnp.exp(piece[0:1] - t_top)
            t_sum = t_sum + piece[2:3] * t_factor
            cross = cross + piece[3:4] * t_factor
            d_sum = d_sum + piece[4:5] * jnp.exp(piece[1:2] - d_top)
            token = token + piece[5:6]
        return t_top, d_top, t_sum, cross, d_sum, token

    place = chip * R + r
    stat_all[place] = pack(stats)
    for dc in (*range(1, half), 0):
        for p in far_first if dc else far_peers:
            device = {"vocab": 2 * lax.rem(chip + dc, half) + core, "req": p}
            copy = describe(
                stat_all.at[place], stat_all.at[place], device, stat_sems.at[place]
            )
            copy.start()
            sent.append(copy)
    got_stats = []
    for dc in range(half):
        for dr in range(R):
            if dc or dr:
                source = lax.rem(chip + dc, half) * R + lax.rem(r + dr, R)
                got_stats.append(incoming(stat_all.at[source], stat_sems.at[source]))
    got_nd_near = push(nd.at[core], nd.at[core], {"vocab": sibling})
    arrive(got_stats)
    t_top, d_top, target_total, cross_total, draft_total, token_logit = combine(
        stat_all, half * R
    )

    row_coef = loss_scale * valid / valid_total
    target_prob = t_pow * to_col(jnp.exp(stats[0] - t_top) / target_total)
    draft_prob = d_pow * to_col(jnp.exp(stats[1] - d_top) / draft_total)
    logit_back = (
        row_coef
        * (
            (1.0 + hard_weight) * draft_prob
            - target_prob
            - jnp.where(onehot, hard_weight, 0.0)
        )
    ).astype(bf16)

    got_b = []
    for p in range(R):
        row_part = None
        for b in range(2):
            term = dot_nt(
                logit_back[:, b * vocab_width : (b + 1) * vocab_width],
                wd[b, p * part : (p + 1) * part],
            )
            row_part = term if row_part is None else row_part + term
        b_out[p] = row_part.reshape(half, rows, part)
        got_b.append(over_chips(lambda c: b_out.at[p, c], b_in.at[p, chip]))
        b_in[p, chip] = b_out[p, chip]
    for b in range(2):
        lb_out[b] = logit_back[:, b * vocab_width : (b + 1) * vocab_width]
    got_lb = push(lb_out.at[1 - core], lb_in.at[core], {"vocab": sibling})
    lb_in[core] = lb_out[core]
    target_lse = t_top + jnp.log(target_total)
    draft_lse = d_top + jnp.log(draft_total)
    row_loss = (
        cross_total / target_total
        - target_lse
        + draft_lse
        + hard_weight * (draft_lse - token_logit)
    )
    loss_all[core] = jnp.broadcast_to(
        jnp.sum(valid_row * row_loss, axis=1, keepdims=True), (8, 128)
    )
    got_loss = push(loss_all.at[core], loss_all.at[core], {"vocab": sibling})
    got_nd_near.wait_recv()
    got_lb.wait_recv()
    lb_all = lb_in[...].reshape(all_rows, vocab_width)
    for p in range(R):
        head_block[p * part : (p + 1) * part] = dot_tn(
            nd[:, :, :, p * part : (p + 1) * part].reshape(all_rows, part), lb_all
        ).astype(bf16)
    head_store = pltpu.make_async_copy(head_block, grad_head, local_sems.at[13])
    head_store.start()

    inner = jnp.zeros((rows, 1), f32)
    for p in range(R):
        arrive(got_b[p])
        piece = total(b_in.at[p], half)
        c_out[p] = piece
        push_unless(p == r, c_out.at[p], c_in.at[r], {"req": p}, c_sems.at[r])
        inner = inner + jnp.sum(piece * gains[p] * hnorm[p], axis=-1, keepdims=True)
    inner_all[r] = jnp.broadcast_to(inner, (rows, 128))
    got_inner = over_req(lambda p: inner_all.at[r], inner_all)

    def c_landed():
        for p in range(R):
            landed(c_in.at[p], c_sems.at[p])

    got_loss.wait_recv()
    mean_loss[...] = (loss_all[0] + loss_all[1])[0:1, 0:1] / valid_total
    arrive(got_inner)
    inner = total(inner_all, R)[:, :1] / width
    c_landed()
    row_back = total(c_in, R)
    norm = hnorm[r]
    out_back = (hidden_scale * (row_back * gains[r] - norm * inner)).astype(bf16)
    ob[v] = out_back
    for k in range(V):
        p = 2 * lax.rem(chip + 1 + k // 2, half) + k % 2
        m_out[p] = dot_nt(out_back, wo[p])
        push_unless(
            jnp.logical_and(p == v, group == r),
            m_out.at[p],
            m_in.at[r],
            {"vocab": p, "req": group},
            m_sems.at[r],
        )

    def m_landed():
        for p in range(R):
            landed(m_in.at[p], m_sems.at[p])

    got_ob = [
        push(ob.at[v], ob.at[v], {"vocab": lax.rem(v + k, V)}) for k in range(1, V)
    ]
    gain_out[...] = jnp.sum(row_back * norm, axis=0, keepdims=True)
    for p in far_first:
        push_unless(
            jnp.logical_and(r == v, p == r),
            gain_out,
            gain_in.at[v],
            {"vocab": r, "req": p},
            gain_sems.at[v],
        )

    def gain_landed():
        for p in range(V):
            landed(gain_in.at[p], gain_sems.at[p])

    flush()
    m_landed()
    mix_back = total(m_in, R).astype(bf16)
    query_parts, key_parts, value_parts = [], [], []
    for s in range(shared):
        back_stack = stack_heads(mix_back, s)
        prob_back = dot_nt(back_stack, values[s])
        delta = jnp.sum(probs[s] * prob_back, axis=-1, keepdims=True)
        score_back = (probs[s] * (prob_back - delta) * inv_root).astype(bf16)
        query_parts.append(dot_nn(score_back, keys[s]))
        key_parts.append(dot_tn(score_back, query_stacks[s]))
        value_parts.append(dot_tn(weights[s], back_stack))
    key_back = jnp.concatenate(key_parts, axis=1)
    key_back = key_back * s_cos - swap_halves(key_back) * s_sin
    kv_out[0] = key_back.astype(kv_out.dtype)
    kv_out[1] = jnp.concatenate(value_parts, axis=1).astype(kv_out.dtype)
    for p in far_first:
        for which in range(2):
            target_v = which * half + chip
            push_unless(
                jnp.logical_and(target_v == v, p == r),
                kv_out.at[which],
                kv_in.at[r, core],
                {"vocab": target_v, "req": p},
                kv_sems.at[r, core],
            )

    def kv_landed():
        for p in range(R):
            for d in range(2):
                landed(kv_in.at[p, d], kv_sems.at[p, d])

    query_back = unstack_heads(query_parts)
    qg[r] = (query_back * q_cos - swap_halves(query_back) * q_sin).astype(bf16)
    got_qg = over_req(lambda p: qg.at[r], qg)

    arrive(got_mix)
    arrive(got_ob)
    grouped(
        lambda g, a, count: mix[g, :, a : a + count],
        lambda g: ob[owner_of(g, V)],
        output_block,
        R,
        128,
    )
    output_store = pltpu.make_async_copy(output_block, grad_output, local_sems.at[14])
    output_store.start()

    gain_landed()
    grad_gain[...] = total(gain_in, V)
    arrive(got_qg)
    query_rows[...] = qg[...]
    kv_landed()
    for p in range(R):
        if pieces == 1:
            keyval_rows[p] = (kv_in[p, 0] + kv_in[p, 1]).astype(bf16)
        else:
            for d in range(2):
                keyval_rows[p, :, d * swidth : (d + 1) * swidth] = kv_in[p, d]
    head_store.wait()
    output_store.wait()
    flush()


def finish_kernel(
    R,
    loss_in,
    head_in,
    gain_in,
    output_in,
    x_in,
    query_in,
    keyval_in,
    mean_loss,
    grad_head,
    grad_gain,
    grad_query,
    grad_keyval,
    grad_output,
    x_rows,
    query_rows,
    keyval_rows,
    head_block,
    output_block,
    query_block,
    keyval_block,
    loss_block,
    gain_block,
    sems,
):
    moves = (
        (x_in, x_rows, None),
        (query_in, query_rows, None),
        (keyval_in, keyval_rows, None),
        (head_in, head_block, grad_head),
        (output_in, output_block, grad_output),
        (loss_in, loss_block, mean_loss),
        (gain_in, gain_block, grad_gain),
        (None, query_block, grad_query),
        (None, keyval_block, grad_keyval),
    )
    loads, stores = [], []
    for k, (source, block, target) in enumerate(moves):
        if source is not None:
            loads.append(pltpu.make_async_copy(source, block, sems.at[0, k]))
            loads[-1].start()
        if target is not None:
            stores.append(pltpu.make_async_copy(block, target, sems.at[1, k]))
    loads[0].wait()
    loads[1].wait()
    grouped(lambda g, a, n: x_rows[g, :, a : a + n], lambda g: query_rows[g], query_block, R, 128)
    stores[4].start()
    for k in range(4):
        loads[3 + k].wait()
        stores[k].start()
    loads[2].wait()
    grouped(lambda g, a, n: x_rows[g, :, a : a + n], lambda g: keyval_rows[g], keyval_block, R, 128)
    stores[5].start()
    for store in stores:
        store.wait()


def shards(
    V,
    R,
    target_hidden,
    target_gain,
    target_head,
    draft_input,
    attn_gain,
    query_proj,
    keyval_proj,
    output_proj,
    draft_gain,
    draft_head,
    parents,
    token_ids,
    valid_counts,
):
    rows, width = draft_input.shape
    part = width // R
    qcols = query_proj.shape[1]
    kcols = keyval_proj.shape[1]
    t_part = target_hidden.shape[1]
    half = V // 2
    vocab_width = draft_head.shape[1]
    gain_width = width // V
    local_heads = qcols // HEAD_DIM
    swidth = max(1, local_heads // (HEADS // KV_HEADS)) * HEAD_DIM
    assert V == R and V % 2 == 0 and output_proj.shape == (qcols, part)
    assert kcols // swidth in (1, 2)
    vm = pl.BlockSpec(memory_space=pltpu.VMEM)
    hbm = pl.BlockSpec(memory_space=pl.ANY)
    buffer = pltpu.VMEM
    outs = pl.pallas_call(
        functools.partial(step_kernel, V, R),
        out_shape=(
            jax.ShapeDtypeStruct((1, 1), f32),
            jax.ShapeDtypeStruct(draft_head.shape, bf16),
            jax.ShapeDtypeStruct((1, gain_width), f32),
            jax.ShapeDtypeStruct(output_proj.shape, bf16),
            jax.ShapeDtypeStruct((R, rows, part), bf16),
            jax.ShapeDtypeStruct((R, rows, qcols), bf16),
            jax.ShapeDtypeStruct((R, rows, kcols), bf16),
        ),
        in_specs=[hbm] * 13,
        out_specs=(vm, hbm, vm, hbm, vm, vm, vm),
        scratch_shapes=[
            buffer(target_hidden.shape, bf16),
            buffer((t_part * V // 128, 128), bf16),
            buffer(draft_input.shape, bf16),
            buffer((width // 128, 128), bf16),
            buffer((width // 128, 128), bf16),
            buffer((1, parents.shape[0]), jnp.int32),
            buffer((1, token_ids.shape[0]), jnp.int32),
            buffer((1, valid_counts.shape[0]), jnp.int32),
            buffer(target_head.shape, bf16),
            buffer(query_proj.shape, bf16),
            buffer(keyval_proj.shape, bf16),
            buffer((2, *draft_head.shape), bf16),
            buffer((V, *output_proj.shape), bf16),
            buffer(draft_head.shape, bf16),
            buffer(output_proj.shape, bf16),
            buffer((1, t_part * V), f32),
            buffer((R, rows, t_part), bf16),
            buffer((V, R, rows, t_part), bf16),
            buffer((R, rows, part), bf16),
            buffer((rows, part), bf16),
            buffer((R, rows, part), bf16),
            buffer((R, rows, part), bf16),
            buffer((kcols // swidth, R, rows, swidth), f32),
            buffer((2, R, rows, swidth), f32),
            buffer((R, rows, qcols), f32),
            buffer((R, rows, qcols), f32),
            buffer((R, rows, qcols), bf16),
            buffer((V, rows, qcols), bf16),
            buffer((R, rows, part), f32),
            buffer((R, rows, part), f32),
            buffer((R, 1, part), f32),
            buffer((2, half, rows, width), bf16),
            buffer((half, rows, 2 * vocab_width), f32),
            buffer((R, rows, vocab_width), f32),
            buffer((2, half, rows, vocab_width), f32),
            buffer((half * R, 8, half * rows), f32),
            buffer((2, 8, 128), f32),
            buffer((2, half * rows, vocab_width), bf16),
            buffer((2, half * rows, vocab_width), bf16),
            buffer((R, half, rows, part), f32),
            buffer((R, half, rows, part), f32),
            buffer((R, rows, part), f32),
            buffer((R, rows, part), f32),
            buffer((R, rows, 128), f32),
            buffer((V, rows, part), bf16),
            buffer((V, rows, qcols), f32),
            buffer((R, rows, qcols), f32),
            buffer((1, part), f32),
            buffer((V, 1, part), f32),
            buffer((2, rows, swidth), f32 if swidth == kcols else bf16),
            buffer((R, 2, rows, swidth), f32 if swidth == kcols else bf16),
            buffer((R, rows, qcols), bf16),
            pltpu.SemaphoreType.DMA((17,)),
            pltpu.SemaphoreType.DMA((20 * R + 8 * V + 2 * half * R + 16,)),
            pltpu.SemaphoreType.DMA((12 * R + 8 * V + half * R + 16,)),
            pltpu.SemaphoreType.DMA((2, R)),
            pltpu.SemaphoreType.DMA((V,)),
            pltpu.SemaphoreType.DMA((R,)),
            pltpu.SemaphoreType.DMA((V,)),
            pltpu.SemaphoreType.DMA((R, 2)),
            pltpu.SemaphoreType.DMA((half * R,)),
            pltpu.SemaphoreType.DMA((R,)),
        ],
        compiler_params=pltpu.CompilerParams(
            collective_id=0, has_side_effects=True, vmem_limit_bytes=56 << 20
        ),
        name="distill_step",
    )(
        target_hidden,
        target_gain.reshape(-1, 128),
        target_head,
        draft_input,
        attn_gain.reshape(-1, 128),
        query_proj,
        keyval_proj,
        output_proj,
        draft_gain.reshape(-1, 128),
        draft_head,
        parents.reshape(1, -1),
        token_ids.reshape(1, -1),
        valid_counts.reshape(1, -1),
    )
    loss, head, gain, query, keyval, output = pl.pallas_call(
        functools.partial(finish_kernel, R),
        out_shape=(
            jax.ShapeDtypeStruct((1, 1), f32),
            jax.ShapeDtypeStruct(draft_head.shape, bf16),
            jax.ShapeDtypeStruct((1, gain_width), f32),
            jax.ShapeDtypeStruct(query_proj.shape, bf16),
            jax.ShapeDtypeStruct(keyval_proj.shape, bf16),
            jax.ShapeDtypeStruct(output_proj.shape, bf16),
        ),
        in_specs=[hbm] * 7,
        out_specs=(hbm,) * 6,
        scratch_shapes=[
            buffer((R, rows, part), bf16),
            buffer((R, rows, qcols), bf16),
            buffer((R, rows, kcols), bf16),
            buffer(draft_head.shape, bf16),
            buffer(output_proj.shape, bf16),
            buffer(query_proj.shape, bf16),
            buffer(keyval_proj.shape, bf16),
            buffer((1, 1), f32),
            buffer((1, gain_width), f32),
            pltpu.SemaphoreType.DMA((2, 9)),
        ],
        name="distill_finish",
    )(*outs)
    return loss.reshape(1), head, gain.reshape(-1), query, keyval, output


def solution(mesh):
    in_specs = (
        P(("job", "req"), "vocab"),
        P("job"),
        P("job", ("vocab", "req")),
        P(("job", "req"), None),
        P("job"),
        P(("job", "req"), "vocab"),
        P(("job", "req"), "vocab"),
        P(("job", "vocab"), "req"),
        P("job"),
        P("job", ("vocab", "req")),
        P(("job", "req")),
        P("job"),
        P("job"),
    )
    out_specs = (
        P("job"),
        P("job", ("vocab", "req")),
        P(("job", "vocab")),
        P(("job", "req"), "vocab"),
        P(("job", "req"), "vocab"),
        P(("job", "vocab"), "req"),
    )
    return jax.shard_map(
        functools.partial(shards, mesh.shape["vocab"], mesh.shape["req"]),
        mesh=mesh,
        in_specs=in_specs,
        out_specs=out_specs,
        check_vma=False,
    )
```

```python
import functools
import math

import jax
import jax.numpy as jnp
from jax import lax
from jax.experimental import pallas as pl
from jax.experimental.pallas import tpu as pltpu
from jax.sharding import PartitionSpec as P

HEADS = 32
KV_HEADS = 8
HEAD_DIM = 64

epsilon = 1e-05
rope_base = 500000.0
hard_weight = 0.5
loss_scale = 1024.0
f32 = jnp.float32
bf16 = jnp.bfloat16
MESH = pl.DeviceIdType.MESH


def dot_nn(a, b):
    return jnp.dot(a, b, preferred_element_type=f32)


def dot_tn(a, b):
    return lax.dot_general(a, b, (((0,), (0,)), ((), ())), preferred_element_type=f32)


def dot_nt(a, b):
    return lax.dot_general(a, b, (((1,), (1,)), ((), ())), preferred_element_type=f32)


def as_row(ref, first, count):
    lanes = ref.shape[1]
    values = ref[...].astype(f32)
    rows = range(first // lanes, (first + count) // lanes)
    return jnp.concatenate([values[k : k + 1] for k in rows], axis=1)


def grouped(lhs, rhs, out, groups, step):
    for first in range(0, out.shape[0], step):
        value = None
        for g in range(groups):
            term = dot_tn(lhs(g, first, step), rhs(g)).astype(bf16).astype(f32)
            value = term if value is None else value + term
        out[first : first + step] = value.astype(bf16)


def total(ref, count):
    value = ref[0]
    for k in range(1, count):
        value = value + ref[k]
    return value


def swap_halves(values):
    width = values.shape[1]
    half = HEAD_DIM // 2
    lane = lax.broadcasted_iota(jnp.int32, values.shape, 1)
    if width % 128 == 0:
        ahead = pltpu.roll(values, width - half, 1)
        behind = pltpu.roll(values, half, 1)
        return jnp.where(lane % HEAD_DIM < half, -ahead, behind)
    pieces = []
    for head in range(width // HEAD_DIM):
        lead = values[:, head * HEAD_DIM : head * HEAD_DIM + half]
        trail = values[:, head * HEAD_DIM + half : (head + 1) * HEAD_DIM]
        pieces += [-trail, lead]
    return jnp.concatenate(pieces, axis=1)


def angles(depth, rows, width):
    lane = lax.broadcasted_iota(jnp.int32, (rows, width), 1) % (HEAD_DIM // 2)
    frequency = jnp.exp(lane.astype(f32) * (-2.0 / HEAD_DIM * math.log(rope_base)))
    return depth * frequency


def group_of(v, V):
    return v // 2 * (1 - v % 2) + (V - 1 - v // 2) * (v % 2)


def owner_of(group, V):
    upper = group // (V // 2)
    return 2 * group * (1 - upper) + (2 * (V - 1 - group) + 1) * upper


def step_kernel(
    V,
    R,
    target_hidden_hbm,
    target_gain_hbm,
    target_head,
    draft_input_hbm,
    attn_gain_hbm,
    query_proj,
    keyval_proj,
    output_proj,
    draft_gain_hbm,
    draft_head,
    parents_hbm,
    token_ids_hbm,
    valid_counts_hbm,
    mean_loss,
    grad_head,
    grad_gain,
    grad_output,
    x_rows,
    query_rows,
    keyval_rows,
    target_hidden,
    target_gain,
    draft_input,
    attn_gain,
    draft_gain,
    parents,
    token_ids,
    valid_counts,
    w_target,
    w_query,
    w_keyval,
    wd,
    wo,
    head_block,
    output_block,
    t_gain,
    t1,
    t2,
    d_out,
    d_in,
    x_out,
    x_in,
    k_out,
    k_in,
    a_out,
    a_in,
    mix,
    hm,
    hid,
    hnorm,
    gains,
    nd,
    dl,
    tl_out,
    tl_in,
    stat_all,
    loss_all,
    lb_out,
    lb_in,
    b_out,
    b_in,
    c_out,
    c_in,
    inner_all,
    ob,
    m_out,
    m_in,
    gain_out,
    gain_in,
    kv_out,
    kv_in,
    qg,
    local_sems,
    send_sems,
    recv_sems,
    k_sems,
    hm_sems,
    m_sems,
    gain_sems,
    kv_sems,
    stat_sems,
    c_sems,
):
    v = lax.axis_index("vocab")
    r = lax.axis_index("req")
    half = V // 2
    chip, core = v // 2, lax.rem(v, 2)
    sibling = v + 1 - 2 * core
    group = group_of(v, V)
    rows, width = draft_input.shape
    all_rows = rows * R
    n = rows * half
    part = width // R
    qcols = query_proj.shape[1]
    kcols = keyval_proj.shape[1]
    vocab_width = draft_head.shape[1]
    t_part = target_hidden.shape[1]
    t_width = t_part * V
    local_heads = qcols // HEAD_DIM
    head_group = HEADS // KV_HEADS
    shared = max(1, local_heads // head_group)
    spread = local_heads // shared
    swidth = shared * HEAD_DIM
    pieces = kcols // swidth
    inv_root = HEAD_DIM ** (-0.5)

    loads = []
    for index, (source, target) in enumerate(
        (
            (draft_input_hbm, draft_input),
            (attn_gain_hbm, attn_gain),
            (query_proj, w_query),
            (keyval_proj, w_keyval),
            (target_head, w_target),
            (output_proj, wo.at[v]),
            (draft_head, wd.at[core]),
            (parents_hbm, parents),
            (target_hidden_hbm, target_hidden),
            (target_gain_hbm, target_gain),
            (draft_gain_hbm, draft_gain),
            (token_ids_hbm, token_ids),
            (valid_counts_hbm, valid_counts),
        )
    ):
        load = pltpu.make_async_copy(source, target, local_sems.at[index])
        load.start()
        loads.append(load)

    def wait_load(index):
        loads[index].wait()

    barrier = pltpu.get_barrier_semaphore()
    for dv in range(V):
        for dr in range(R):
            if dv or dr:
                pl.semaphore_signal(
                    barrier,
                    inc=1,
                    device_id={"vocab": lax.rem(v + dv, V), "req": lax.rem(r + dr, R)},
                    device_id_type=MESH,
                )

    sent, sent_unless = [], []
    used = [0, 0]

    def flush():
        for copy in sent:
            copy.wait_send()
        for copy, here in sent_unless:

            @pl.when(jnp.logical_not(here))
            def _():
                copy.wait_send()

        sent.clear()
        sent_unless.clear()

    def describe(source, target, device, recv):
        used[0] += 1
        return pltpu.make_async_remote_copy(
            src_ref=source,
            dst_ref=target,
            send_sem=send_sems.at[used[0] - 1],
            recv_sem=recv,
            device_id=device,
            device_id_type=MESH,
        )

    def push(source, target, device, recv=None):
        if recv is None:
            recv = recv_sems.at[used[1]]
            used[1] += 1
        copy = describe(source, target, device, recv)
        copy.start()
        sent.append(copy)
        return copy

    def push_unless(here, source, target, device, recv):
        copy = describe(source, target, device, recv)

        @pl.when(jnp.logical_not(here))
        def _():
            copy.start()

        @pl.when(here)
        def _():
            pltpu.make_async_copy(source, target, recv).start()

        sent_unless.append((copy, here))

    def incoming(target, recv):
        return pltpu.make_async_remote_copy(
            src_ref=target,
            dst_ref=target,
            send_sem=recv,
            recv_sem=recv,
            device_id={"vocab": sibling},
            device_id_type=MESH,
        )

    def landed(target, recv):
        incoming(target, recv).wait_recv()

    low = 1 - r // (R // 2)
    far_first = [low * (R - 1 - k) + (1 - low) * k for k in range(R)]
    far_peers = [
        low * (R - 2 - k + (2 * R - 2 - k - r) // R)
        + (1 - low) * (k + 1 - (r - k + R - 1) // R)
        for k in range(R - 1)
    ]

    def over_req(source, target):
        first = used[1]
        used[1] += R
        for k in range(1, R):
            p = lax.rem(r + k, R)
            copy = describe(source(p), target.at[r], {"req": p}, recv_sems.at[first + r])
            copy.start()
            sent.append(copy)
        arrivals = []
        for k in range(1, R):
            p = lax.rem(r + k, R)
            arrivals.append(incoming(target.at[p], recv_sems.at[first + p]))
        return arrivals

    def over_chips(source, target):
        chips = [lax.rem(chip + k, half) for k in range(1, half)]
        return [push(source(c), target, {"vocab": 2 * c + core}) for c in chips]

    def arrive(copies):
        for copy in copies:
            copy.wait_recv()

    wait_load(0)
    wait_load(1)
    inputs = draft_input[...].astype(f32)
    scale = lax.rsqrt(jnp.mean(inputs * inputs, axis=-1, keepdims=True) + epsilon)
    normed = (inputs * scale * as_row(attn_gain, 0, width)).astype(bf16)
    for p in range(R):
        x_out[p] = normed[:, p * part : (p + 1) * part]
    x_in[r] = x_out[r]

    pl.semaphore_wait(barrier, V * R - 1)
    got_x = over_req(lambda p: x_out.at[p], x_in)
    wait_load(8)
    t1[r] = target_hidden[...]
    got_t1 = over_req(lambda p: t1.at[r], t1)
    early = qcols * 3 // 8

    def wo_block(slot, first, last):
        return wo.at[slot, pl.ds(first, last - first)]

    got_wo = over_chips(
        lambda c: output_proj.at[:early], wo_block(v, 0, early)
    )
    got_wd = push(draft_head, wd.at[core], {"vocab": sibling})
    for p in range(R):
        d_out[p] = draft_input[:, p * part : (p + 1) * part]
    here = r == group
    for p in far_peers:
        copy = describe(d_out.at[p], d_in, {"req": p}, local_sems.at[16])

        @pl.when(here)
        def _():
            copy.start()

        sent_unless.append((copy, jnp.logical_not(here)))

    @pl.when(here)
    def _():
        d_in[...] = d_out[r]

    def d_landed():
        @pl.when(r != group)
        def _():
            landed(d_in, local_sems.at[16])

    wait_load(7)
    row_i = lax.broadcasted_iota(jnp.int32, (rows, rows), 0)
    col_i = lax.broadcasted_iota(jnp.int32, (rows, rows), 1)
    eye = row_i == col_i
    parent_col = jnp.sum(
        jnp.where(eye, parents[...].astype(f32), 0.0), axis=1, keepdims=True
    )
    linked = jnp.where(
        jnp.logical_or(eye, parent_col == col_i.astype(f32)), 1.0, 0.0
    ).astype(f32)
    for doubling in range(max(1, (rows - 1).bit_length())):
        half_linked = linked.astype(bf16)
        linked = jnp.minimum(dot_nn(half_linked, half_linked), 1.0)
    depth = jnp.sum(linked, axis=1, keepdims=True) - 1.0
    table = min(qcols, 128)
    angle = angles(depth, rows, table)
    q_cos = jnp.concatenate([jnp.cos(angle)] * (qcols // table), axis=1)
    q_sin = jnp.concatenate([jnp.sin(angle)] * (qcols // table), axis=1)
    s_cos, s_sin = q_cos[:, :swidth], q_sin[:, :swidth]

    wait_load(3)
    arrive(got_x)
    x_all = x_in[...].reshape(all_rows, part)
    kv_part = dot_nn(x_all, w_keyval[...])
    for piece in range(pieces):
        k_out[piece] = kv_part[:, piece * swidth : (piece + 1) * swidth].reshape(
            R, rows, swidth
        )
    kind = v // half
    for p in far_first:
        for d in range(2):
            target_v = lax.rem(v, half) * 2 + d
            push_unless(
                jnp.logical_and(target_v == v, p == r),
                k_out.at[d * pieces // 2, p],
                k_in.at[kind, r],
                {"vocab": target_v, "req": p},
                k_sems.at[kind, r],
            )

    def k_landed():
        for p in range(R):
            for which in range(2):
                landed(k_in.at[which, p], k_sems.at[which, p])

    got_wo_late = over_chips(
        lambda c: output_proj.at[early:], wo_block(v, early, qcols)
    )
    wait_load(2)
    a_out[...] = dot_nn(x_all, w_query[...]).reshape(R, rows, qcols)
    got_a = over_req(lambda p: a_out.at[p], a_in)
    a_in[r] = a_out[r]
    got_wo_near = push(output_proj, wo.at[v], {"vocab": sibling})
    x_rows[...] = x_in[...]

    wait_load(10)
    wait_load(9)
    wait_load(11)
    wait_load(12)
    for p in range(R):
        gains[p] = as_row(draft_gain, p * part, part)
    t_gain[...] = as_row(target_gain, 0, t_width)

    big_row = lax.broadcasted_iota(jnp.int32, (n, n), 0)
    big_col = lax.broadcasted_iota(jnp.int32, (n, n), 1)
    diagonal = big_row == big_col

    def to_col(row):
        return jnp.sum(jnp.where(diagonal, row, 0.0), axis=1, keepdims=True)

    def to_row(col):
        return jnp.sum(jnp.where(diagonal, col, 0.0), axis=0, keepdims=True)

    def groups_of(index):
        place = index // rows
        return place * (1 - core) + (V - 1 - place) * core

    token_row = lax.broadcasted_iota(jnp.int32, (n, all_rows), 0)
    token_at = lax.broadcasted_iota(jnp.int32, (n, all_rows), 1)
    token_col = jnp.sum(
        jnp.where(
            groups_of(token_row) * rows + token_row % rows == token_at,
            token_ids[...].astype(f32),
            0.0,
        ),
        axis=1,
        keepdims=True,
    )
    lane = lax.broadcasted_iota(jnp.int32, (n, 2 * vocab_width), 1)
    lane_block = lane // vocab_width
    columns = ((2 * chip + lane_block) * R + r) * vocab_width + lane % vocab_width
    onehot = token_col == columns.astype(f32)
    counts = valid_counts[...].astype(f32)
    group_row = lax.broadcasted_iota(jnp.int32, (n, R), 0)
    group_col = lax.broadcasted_iota(jnp.int32, (n, R), 1)
    count_col = jnp.sum(
        jnp.where(groups_of(group_row) == group_col, counts, 0.0), axis=1, keepdims=True
    )
    local_row = (lax.broadcasted_iota(jnp.int32, (n, 1), 0) % rows).astype(f32)
    valid = jnp.where(local_row < count_col, 1.0, 0.0)
    valid_row = to_row(valid)
    valid_total = jnp.sum(counts, axis=1, keepdims=True)

    k_landed()
    key_raw = total(k_in.at[0], R)
    key_rows = (key_raw * s_cos + swap_halves(key_raw) * s_sin).astype(bf16)
    value_rows = total(k_in.at[1], R).astype(bf16)
    arrive(got_a)
    query_raw = total(a_in, R)
    queries = (query_raw * q_cos + swap_halves(query_raw) * q_sin).astype(bf16)

    def stack_heads(values, group):
        return jnp.concatenate(
            [
                values[:, (group * spread + h) * HEAD_DIM : (group * spread + h + 1) * HEAD_DIM]
                for h in range(spread)
            ],
            axis=0,
        )

    def unstack_heads(stacks):
        return jnp.concatenate(
            [stack[h * rows : (h + 1) * rows] for stack in stacks for h in range(spread)],
            axis=1,
        )

    query_stacks = [stack_heads(queries, s) for s in range(shared)]
    allowed = jnp.concatenate([linked] * spread, axis=0) > 0.5
    probs, weights, keys, values, mixes = [], [], [], [], []
    for s in range(shared):
        key = key_rows[:, s * HEAD_DIM : (s + 1) * HEAD_DIM]
        value = value_rows[:, s * HEAD_DIM : (s + 1) * HEAD_DIM]
        scores = dot_nt(query_stacks[s], key) * inv_root
        scores = jnp.where(allowed, scores, -jnp.inf)
        powers = jnp.exp(scores - jnp.max(scores, axis=-1, keepdims=True))
        prob = powers / jnp.sum(powers, axis=-1, keepdims=True)
        weight = prob.astype(bf16)
        probs.append(prob)
        weights.append(weight)
        keys.append(key)
        values.append(value)
        mixes.append(dot_nn(weight, value))
    mix[r] = unstack_heads(mixes).astype(bf16)
    owner = owner_of(r, V)
    for p in far_first:
        push_unless(
            jnp.logical_and(owner == v, p == r),
            mix.at[r],
            hm.at[v],
            {"vocab": owner, "req": p},
            hm_sems.at[v],
        )

    def hm_landed():
        for p in range(V):
            landed(hm.at[p], hm_sems.at[p])

    got_wo_pass = []
    for copies, low, high in ((got_wo, 0, early), (got_wo_late, early, qcols)):
        arrive(copies)
        for k in range(1, half):
            sender = lax.rem(v + V - 2 * k, V)
            got_wo_pass.append(
                push(wo_block(sender, low, high), wo_block(sender, low, high), {"vocab": sibling})
            )
    arrive(got_t1)
    t2[v] = t1[...]
    got_t2_far = over_chips(lambda c: t2.at[v], t2.at[v])
    got_t2_near = push(t2.at[v], t2.at[v], {"vocab": sibling})
    got_mix = over_req(lambda p: mix.at[r], mix)

    wait_load(5)
    got_wo_near.wait_recv()
    d_landed()
    value = d_in[...].astype(f32)
    hm_landed()
    arrive(got_wo_pass)
    attn_out = None
    for p in range(V):
        term = dot_nn(hm[p], wo[p])
        attn_out = term if attn_out is None else attn_out + term
    hid[r] = value + attn_out
    got_h = over_req(lambda p: hid.at[r], hid)

    arrive(got_t2_far)
    got_pass = []
    for k in range(1, half):
        sender = lax.rem(v + V - 2 * k, V)
        got_pass.append(push(t2.at[sender], t2.at[sender], {"vocab": sibling}))
    wait_load(4)
    got_t2_near.wait_recv()
    arrive(got_pass)
    squares = jnp.zeros((all_rows, 1), f32)
    for p in range(V):
        piece = t2[p].reshape(all_rows, t_part).astype(f32)
        squares = squares + jnp.sum(piece * piece, axis=-1, keepdims=True)
    t_scale = lax.rsqrt(squares / t_width + epsilon)

    def target_part(first, last):
        value = None
        for p in range(first, last):
            piece = t2[p].reshape(all_rows, t_part).astype(f32)
            piece = (piece * t_scale * t_gain[:, p * t_part : (p + 1) * t_part]).astype(bf16)
            term = dot_nn(piece, w_target[p * t_part : (p + 1) * t_part])
            value = term if value is None else value + term
        return value

    first_logits = target_part(0, half)

    arrive(got_h)
    squares = jnp.zeros((rows, 1), f32)
    for p in range(R):
        squares = squares + jnp.sum(hid[p] * hid[p], axis=-1, keepdims=True)
    hidden_scale = lax.rsqrt(squares / width + epsilon)
    got_nd = []
    for p in range(R):
        norm = hid[p] * hidden_scale
        hnorm[p] = norm
        nd[core, chip, :, p * part : (p + 1) * part] = (norm * gains[p]).astype(bf16)
        if (p + 1) * 2 % R == 0:
            block = nd.at[core, chip, :, (p + 1) * part - width // 2 : (p + 1) * part]
            got_nd += over_chips(lambda c: block, block)
    tl_out[...] = (first_logits + target_part(half, V)).reshape(R, rows, vocab_width)
    got_tl = []
    for k in range(half):
        mine = k * (1 - core) + (V - 1 - k) * core
        other = k * core + (V - 1 - k) * (1 - core)
        got_tl.append(push(tl_out.at[other], tl_in.at[core, k], {"vocab": sibling}))
        tl_in[core, k] = tl_out[mine]
    wait_load(6)
    got_wd.wait_recv()

    def draft_part(place):
        for b in range(2):
            dl[place, :, b * vocab_width : (b + 1) * vocab_width] = dot_nn(
                nd[core, place], wd[b]
            )

    draft_part(chip)
    arrive(got_tl)
    target_logits = jnp.concatenate(
        [tl_in[b].reshape(n, vocab_width) for b in range(2)], axis=1
    )
    t_max = jnp.max(target_logits, axis=1, keepdims=True)
    t_pow = jnp.exp(target_logits - t_max)
    t_sum = jnp.sum(t_pow, axis=1, keepdims=True)
    arrive(got_nd)
    for k in range(1, half):
        draft_part(lax.rem(chip + k, half))

    draft_logits = dl[...].reshape(n, 2 * vocab_width)
    d_max = jnp.max(draft_logits, axis=1, keepdims=True)
    d_pow = jnp.exp(draft_logits - d_max)
    stats = (
        t_max,
        d_max,
        t_sum,
        jnp.sum(t_pow * (target_logits - draft_logits), axis=1, keepdims=True),
        jnp.sum(d_pow, axis=1, keepdims=True),
        jnp.sum(jnp.where(onehot, draft_logits, 0.0), axis=1, keepdims=True),
    )
    stats = [to_row(item) for item in stats]
    stat_kind = lax.broadcasted_iota(jnp.int32, (8, n), 0)

    def pack(items):
        packed = jnp.zeros((8, n), f32)
        for index, item in enumerate(items):
            packed = jnp.where(stat_kind == index, item, packed)
        return packed

    def combine(ref, count):
        top = ref[0]
        for k in range(1, count):
            top = jnp.maximum(top, ref[k])
        t_top, d_top = top[0:1], top[1:2]
        t_sum, cross, d_sum, token = 0.0, 0.0, 0.0, 0.0
        for k in range(count):
            piece = ref[k]
            t_factor = jnp.exp(piece[0:1] - t_top)
            t_sum = t_sum + piece[2:3] * t_factor
            cross = cross + piece[3:4] * t_factor
            d_sum = d_sum + piece[4:5] * jnp.exp(piece[1:2] - d_top)
            token = token + piece[5:6]
        return t_top, d_top, t_sum, cross, d_sum, token

    place = chip * R + r
    stat_all[place] = pack(stats)
    for dc in (*range(1, half), 0):
        for p in far_first if dc else far_peers:
            device = {"vocab": 2 * lax.rem(chip + dc, half) + core, "req": p}
            copy = describe(
                stat_all.at[place], stat_all.at[place], device, stat_sems.at[place]
            )
            copy.start()
            sent.append(copy)
    got_stats = []
    for dc in range(half):
        for dr in range(R):
            if dc or dr:
                source = lax.rem(chip + dc, half) * R + lax.rem(r + dr, R)
                got_stats.append(incoming(stat_all.at[source], stat_sems.at[source]))
    got_nd_near = push(nd.at[core], nd.at[core], {"vocab": sibling})
    arrive(got_stats)
    t_top, d_top, target_total, cross_total, draft_total, token_logit = combine(
        stat_all, half * R
    )

    row_coef = loss_scale * valid / valid_total
    target_prob = t_pow * to_col(jnp.exp(stats[0] - t_top) / target_total)
    draft_prob = d_pow * to_col(jnp.exp(stats[1] - d_top) / draft_total)
    logit_back = (
        row_coef
        * (
            (1.0 + hard_weight) * draft_prob
            - target_prob
            - jnp.where(onehot, hard_weight, 0.0)
        )
    ).astype(bf16)

    got_b = []
    own_last = [lax.rem(r + 1 + k, R) for k in range(R)]
    for p in own_last:
        row_part = None
        for b in range(2):
            term = dot_nt(
                logit_back[:, b * vocab_width : (b + 1) * vocab_width],
                wd[b, pl.ds(pl.multiple_of(p * part, part), part)],
            )
            row_part = term if row_part is None else row_part + term
        b_out[p] = row_part.reshape(half, rows, part)
        got_b.append(over_chips(lambda c: b_out.at[p, c], b_in.at[p, chip]))
        b_in[p, chip] = b_out[p, chip]
    for b in range(2):
        lb_out[b] = logit_back[:, b * vocab_width : (b + 1) * vocab_width]
    got_lb = push(lb_out.at[1 - core], lb_in.at[core], {"vocab": sibling})
    lb_in[core] = lb_out[core]
    target_lse = t_top + jnp.log(target_total)
    draft_lse = d_top + jnp.log(draft_total)
    row_loss = (
        cross_total / target_total
        - target_lse
        + draft_lse
        + hard_weight * (draft_lse - token_logit)
    )
    loss_all[core] = jnp.broadcast_to(
        jnp.sum(valid_row * row_loss, axis=1, keepdims=True), (8, 128)
    )
    got_loss = push(loss_all.at[core], loss_all.at[core], {"vocab": sibling})
    got_nd_near.wait_recv()
    got_lb.wait_recv()
    lb_all = lb_in[...].reshape(all_rows, vocab_width)
    for p in range(R):
        head_block[p * part : (p + 1) * part] = dot_tn(
            nd[:, :, :, p * part : (p + 1) * part].reshape(all_rows, part), lb_all
        ).astype(bf16)
    head_store = pltpu.make_async_copy(head_block, grad_head, local_sems.at[13])
    head_store.start()

    inner = jnp.zeros((rows, 1), f32)
    for k, p in enumerate(own_last):
        arrive(got_b[k])
        piece = total(b_in.at[p], half)
        c_out[p] = piece
        push_unless(p == r, c_out.at[p], c_in.at[r], {"req": p}, c_sems.at[r])
        inner = inner + jnp.sum(piece * gains[p] * hnorm[p], axis=-1, keepdims=True)
    wide = jnp.broadcast_to(inner, (rows, 128))
    inner_lane = lax.broadcasted_iota(jnp.int32, (rows // 2, 128), 1)
    inner_all[r] = jnp.where(inner_lane < 64, wide[: rows // 2], wide[rows // 2 :])
    got_inner = over_req(lambda p: inner_all.at[r], inner_all)

    def c_landed():
        for p in range(R):
            landed(c_in.at[p], c_sems.at[p])

    got_loss.wait_recv()
    mean_loss[...] = (loss_all[0] + loss_all[1])[0:1, 0:1] / valid_total
    arrive(got_inner)
    inner = total(inner_all, R)
    inner = jnp.concatenate([inner[:, :1], inner[:, 64:65]], axis=0) / width
    c_landed()
    row_back = total(c_in, R)
    norm = hnorm[r]
    out_back = (hidden_scale * (row_back * gains[r] - norm * inner)).astype(bf16)
    ob[v] = out_back
    for k in range(V):
        p = 2 * lax.rem(chip + 1 + k // 2, half) + k % 2
        m_out[p] = dot_nt(out_back, wo[p])
        push_unless(
            jnp.logical_and(p == v, group == r),
            m_out.at[p],
            m_in.at[r],
            {"vocab": p, "req": group},
            m_sems.at[r],
        )

    def m_landed():
        for p in range(R):
            landed(m_in.at[p], m_sems.at[p])

    got_ob = [
        push(ob.at[v], ob.at[v], {"vocab": lax.rem(v + k, V)}) for k in range(1, V)
    ]
    gain_out[...] = jnp.sum(row_back * norm, axis=0, keepdims=True)
    for p in far_first:
        push_unless(
            jnp.logical_and(r == v, p == r),
            gain_out,
            gain_in.at[v],
            {"vocab": r, "req": p},
            gain_sems.at[v],
        )

    def gain_landed():
        for p in range(V):
            landed(gain_in.at[p], gain_sems.at[p])

    flush()
    m_landed()
    mix_back = total(m_in, R).astype(bf16)
    query_parts, key_parts, value_parts = [], [], []
    for s in range(shared):
        back_stack = stack_heads(mix_back, s)
        prob_back = dot_nt(back_stack, values[s])
        delta = jnp.sum(probs[s] * prob_back, axis=-1, keepdims=True)
        score_back = (probs[s] * (prob_back - delta) * inv_root).astype(bf16)
        query_parts.append(dot_nn(score_back, keys[s]))
        key_parts.append(dot_tn(score_back, query_stacks[s]))
        value_parts.append(dot_tn(weights[s], back_stack))
    key_back = jnp.concatenate(key_parts, axis=1)
    key_back = key_back * s_cos - swap_halves(key_back) * s_sin
    kv_out[0] = key_back.astype(kv_out.dtype)
    kv_out[1] = jnp.concatenate(value_parts, axis=1).astype(kv_out.dtype)
    for p in far_first:
        for which in range(2):
            target_v = which * half + chip
            push_unless(
                jnp.logical_and(target_v == v, p == r),
                kv_out.at[which],
                kv_in.at[r, core],
                {"vocab": target_v, "req": p},
                kv_sems.at[r, core],
            )

    def kv_landed():
        for p in range(R):
            for d in range(2):
                landed(kv_in.at[p, d], kv_sems.at[p, d])

    query_back = unstack_heads(query_parts)
    qg[r] = (query_back * q_cos - swap_halves(query_back) * q_sin).astype(bf16)
    got_qg = over_req(lambda p: qg.at[r], qg)

    arrive(got_mix)
    arrive(got_ob)
    grouped(
        lambda g, a, count: mix[g, :, a : a + count],
        lambda g: ob[owner_of(g, V)],
        output_block,
        R,
        128,
    )
    output_store = pltpu.make_async_copy(output_block, grad_output, local_sems.at[14])
    output_store.start()

    gain_landed()
    grad_gain[...] = total(gain_in, V)
    arrive(got_qg)
    query_rows[...] = qg[...]
    kv_landed()
    for p in range(R):
        if pieces == 1:
            keyval_rows[p] = (kv_in[p, 0] + kv_in[p, 1]).astype(bf16)
        else:
            for d in range(2):
                keyval_rows[p, :, d * swidth : (d + 1) * swidth] = kv_in[p, d]
    head_store.wait()
    output_store.wait()
    flush()


def finish_kernel(
    R,
    loss_in,
    head_in,
    gain_in,
    output_in,
    x_in,
    query_in,
    keyval_in,
    mean_loss,
    grad_head,
    grad_gain,
    grad_query,
    grad_keyval,
    grad_output,
    x_rows,
    query_rows,
    keyval_rows,
    head_block,
    output_block,
    query_block,
    keyval_block,
    loss_block,
    gain_block,
    sems,
):
    moves = (
        (x_in, x_rows, None),
        (query_in, query_rows, None),
        (keyval_in, keyval_rows, None),
        (head_in, head_block, grad_head),
        (output_in, output_block, grad_output),
        (loss_in, loss_block, mean_loss),
        (gain_in, gain_block, grad_gain),
        (None, query_block, grad_query),
        (None, keyval_block, grad_keyval),
    )
    loads, stores = [], []
    for k, (source, block, target) in enumerate(moves):
        if source is not None:
            loads.append(pltpu.make_async_copy(source, block, sems.at[0, k]))
            loads[-1].start()
        if target is not None:
            stores.append(pltpu.make_async_copy(block, target, sems.at[1, k]))
    loads[0].wait()
    loads[1].wait()
    grouped(lambda g, a, n: x_rows[g, :, a : a + n], lambda g: query_rows[g], query_block, R, 128)
    stores[4].start()
    for k in range(4):
        loads[3 + k].wait()
        stores[k].start()
    loads[2].wait()
    grouped(lambda g, a, n: x_rows[g, :, a : a + n], lambda g: keyval_rows[g], keyval_block, R, 128)
    stores[5].start()
    for store in stores:
        store.wait()


def shards(
    V,
    R,
    target_hidden,
    target_gain,
    target_head,
    draft_input,
    attn_gain,
    query_proj,
    keyval_proj,
    output_proj,
    draft_gain,
    draft_head,
    parents,
    token_ids,
    valid_counts,
):
    rows, width = draft_input.shape
    part = width // R
    qcols = query_proj.shape[1]
    kcols = keyval_proj.shape[1]
    t_part = target_hidden.shape[1]
    half = V // 2
    vocab_width = draft_head.shape[1]
    gain_width = width // V
    local_heads = qcols // HEAD_DIM
    swidth = max(1, local_heads // (HEADS // KV_HEADS)) * HEAD_DIM
    assert V == R and V % 2 == 0 and output_proj.shape == (qcols, part)
    assert kcols // swidth in (1, 2)
    vm = pl.BlockSpec(memory_space=pltpu.VMEM)
    hbm = pl.BlockSpec(memory_space=pl.ANY)
    buffer = pltpu.VMEM
    outs = pl.pallas_call(
        functools.partial(step_kernel, V, R),
        out_shape=(
            jax.ShapeDtypeStruct((1, 1), f32),
            jax.ShapeDtypeStruct(draft_head.shape, bf16),
            jax.ShapeDtypeStruct((1, gain_width), f32),
            jax.ShapeDtypeStruct(output_proj.shape, bf16),
            jax.ShapeDtypeStruct((R, rows, part), bf16),
            jax.ShapeDtypeStruct((R, rows, qcols), bf16),
            jax.ShapeDtypeStruct((R, rows, kcols), bf16),
        ),
        in_specs=[hbm] * 13,
        out_specs=(vm, hbm, vm, hbm, vm, vm, vm),
        scratch_shapes=[
            buffer(target_hidden.shape, bf16),
            buffer((t_part * V // 128, 128), bf16),
            buffer(draft_input.shape, bf16),
            buffer((width // 128, 128), bf16),
            buffer((width // 128, 128), bf16),
            buffer((1, parents.shape[0]), jnp.int32),
            buffer((1, token_ids.shape[0]), jnp.int32),
            buffer((1, valid_counts.shape[0]), jnp.int32),
            buffer(target_head.shape, bf16),
            buffer(query_proj.shape, bf16),
            buffer(keyval_proj.shape, bf16),
            buffer((2, *draft_head.shape), bf16),
            buffer((V, *output_proj.shape), bf16),
            buffer(draft_head.shape, bf16),
            buffer(output_proj.shape, bf16),
            buffer((1, t_part * V), f32),
            buffer((R, rows, t_part), bf16),
            buffer((V, R, rows, t_part), bf16),
            buffer((R, rows, part), bf16),
            buffer((rows, part), bf16),
            buffer((R, rows, part), bf16),
            buffer((R, rows, part), bf16),
            buffer((kcols // swidth, R, rows, swidth), f32),
            buffer((2, R, rows, swidth), f32),
            buffer((R, rows, qcols), f32),
            buffer((R, rows, qcols), f32),
            buffer((R, rows, qcols), bf16),
            buffer((V, rows, qcols), bf16),
            buffer((R, rows, part), f32),
            buffer((R, rows, part), f32),
            buffer((R, 1, part), f32),
            buffer((2, half, rows, width), bf16),
            buffer((half, rows, 2 * vocab_width), f32),
            buffer((R, rows, vocab_width), f32),
            buffer((2, half, rows, vocab_width), f32),
            buffer((half * R, 8, half * rows), f32),
            buffer((2, 8, 128), f32),
            buffer((2, half * rows, vocab_width), bf16),
            buffer((2, half * rows, vocab_width), bf16),
            buffer((R, half, rows, part), f32),
            buffer((R, half, rows, part), f32),
            buffer((R, rows, part), f32),
            buffer((R, rows, part), f32),
            buffer((R, rows // 2, 128), f32),
            buffer((V, rows, part), bf16),
            buffer((V, rows, qcols), f32),
            buffer((R, rows, qcols), f32),
            buffer((1, part), f32),
            buffer((V, 1, part), f32),
            buffer((2, rows, swidth), f32 if swidth == kcols else bf16),
            buffer((R, 2, rows, swidth), f32 if swidth == kcols else bf16),
            buffer((R, rows, qcols), bf16),
            pltpu.SemaphoreType.DMA((17,)),
            pltpu.SemaphoreType.DMA((20 * R + 8 * V + 2 * half * R + 16,)),
            pltpu.SemaphoreType.DMA((12 * R + 8 * V + half * R + 16,)),
            pltpu.SemaphoreType.DMA((2, R)),
            pltpu.SemaphoreType.DMA((V,)),
            pltpu.SemaphoreType.DMA((R,)),
            pltpu.SemaphoreType.DMA((V,)),
            pltpu.SemaphoreType.DMA((R, 2)),
            pltpu.SemaphoreType.DMA((half * R,)),
            pltpu.SemaphoreType.DMA((R,)),
        ],
        compiler_params=pltpu.CompilerParams(
            collective_id=0, has_side_effects=True, vmem_limit_bytes=56 << 20
        ),
        name="distill_step",
    )(
        target_hidden,
        target_gain.reshape(-1, 128),
        target_head,
        draft_input,
        attn_gain.reshape(-1, 128),
        query_proj,
        keyval_proj,
        output_proj,
        draft_gain.reshape(-1, 128),
        draft_head,
        parents.reshape(1, -1),
        token_ids.reshape(1, -1),
        valid_counts.reshape(1, -1),
    )
    loss, head, gain, query, keyval, output = pl.pallas_call(
        functools.partial(finish_kernel, R),
        out_shape=(
            jax.ShapeDtypeStruct((1, 1), f32),
            jax.ShapeDtypeStruct(draft_head.shape, bf16),
            jax.ShapeDtypeStruct((1, gain_width), f32),
            jax.ShapeDtypeStruct(query_proj.shape, bf16),
            jax.ShapeDtypeStruct(keyval_proj.shape, bf16),
            jax.ShapeDtypeStruct(output_proj.shape, bf16),
        ),
        in_specs=[hbm] * 7,
        out_specs=(hbm,) * 6,
        scratch_shapes=[
            buffer((R, rows, part), bf16),
            buffer((R, rows, qcols), bf16),
            buffer((R, rows, kcols), bf16),
            buffer(draft_head.shape, bf16),
            buffer(output_proj.shape, bf16),
            buffer(query_proj.shape, bf16),
            buffer(keyval_proj.shape, bf16),
            buffer((1, 1), f32),
            buffer((1, gain_width), f32),
            pltpu.SemaphoreType.DMA((2, 9)),
        ],
        name="distill_finish",
    )(*outs)
    return loss.reshape(1), head, gain.reshape(-1), query, keyval, output


def solution(mesh):
    in_specs = (
        P(("job", "req"), "vocab"),
        P("job"),
        P("job", ("vocab", "req")),
        P(("job", "req"), None),
        P("job"),
        P(("job", "req"), "vocab"),
        P(("job", "req"), "vocab"),
        P(("job", "vocab"), "req"),
        P("job"),
        P("job", ("vocab", "req")),
        P(("job", "req")),
        P("job"),
        P("job"),
    )
    out_specs = (
        P("job"),
        P("job", ("vocab", "req")),
        P(("job", "vocab")),
        P(("job", "req"), "vocab"),
        P(("job", "req"), "vocab"),
        P(("job", "vocab"), "req"),
    )
    return jax.shard_map(
        functools.partial(shards, mesh.shape["vocab"], mesh.shape["req"]),
        mesh=mesh,
        in_specs=in_specs,
        out_specs=out_specs,
        check_vma=False,
    )
```
